32 devices in a mesh: dp: 4 (over z), row: 2 (over core), col: 4 (over y, x).
Axes of the slice: x: 2, y: 2, z: 4, core: 2. Of those that a mesh axis runs over, the one named last changes fastest.
Arguments:
- residual_in: float32 [2048, 1024], P('dp', ('row', 'col')), may hold values from -6 to 6
- positions: int32 [2048], P('dp'), may hold values from 0 to 511, as said below
- attn_gain: float32 [2, 1024], P(None, ('row', 'col')), may hold values from 0.1 to 1.9
- query_weight: bfloat16 [2, 1024, 2048], P(None, 'row', 'col'), may hold values from -0.1875 to 0.1875
- key_weight: bfloat16 [2, 1024, 1024], P(None, 'row', 'col'), may hold values from -0.1875 to 0.1875
- value_weight: bfloat16 [2, 1024, 1024], P(None, 'row', 'col'), may hold values from -0.1875 to 0.1875
- query_gain: float32 [2, 128], replicated, may hold values from 0.1 to 1.9
- key_gain: float32 [2, 128], replicated, may hold values from 0.1 to 1.9
- output_weight: bfloat16 [2, 2048, 1024], P(None, 'col', 'row'), may hold values from -1 to 1
- ffn_gain: float32 [2, 1024], P(None, ('row', 'col')), may hold values from 0.1 to 1.9
- gate_weight: bfloat16 [2, 1024, 3072], P(None, 'row', 'col'), may hold values from -0.1875 to 0.1875
- up_weight: bfloat16 [2, 1024, 3072], P(None, 'row', 'col'), may hold values from -0.1875 to 0.1875
- down_weight: bfloat16 [2, 3072, 1024], P(None, 'col', 'row'), may hold values from -0.109375 to 0.109375
- output_grad: float32 [2048, 1024], P('dp', ('row', 'col')), may hold values from -6 to 6
Outputs:
- outputs: float32 [2048, 1024], P('dp', ('row', 'col'))
- input_grad: float32 [2048, 1024], P('dp', ('row', 'col'))
- attn_gain_grad: float32 [2, 1024], P(None, ('row', 'col'))
- query_weight_grad: float32 [2, 1024, 2048], P(None, 'row', 'col')
- key_weight_grad: float32 [2, 1024, 1024], P(None, 'row', 'col')
- value_weight_grad: float32 [2, 1024, 1024], P(None, 'row', 'col')
- query_gain_grad: float32 [2, 128], replicated
- key_gain_grad: float32 [2, 128], replicated
- output_weight_grad: float32 [2, 2048, 1024], P(None, 'col', 'row')
- ffn_gain_grad: float32 [2, 1024], P(None, ('row', 'col'))
- gate_weight_grad: float32 [2, 1024, 3072], P(None, 'row', 'col')
- up_weight_grad: float32 [2, 1024, 3072], P(None, 'row', 'col')
- down_weight_grad: float32 [2, 3072, 1024], P(None, 'col', 'row')
The draws below stay inside these ranges and needn't reach their ends.
Inputs may be any that keep to these rules, and one draw needn't show every extreme that they name: `positions`: within each sequence of 512 tokens, the first position is 0 and each later one is either 0 or one more than the one before.
All inputs are finite; a program needn't handle non-finite values.
Results may differ from the reference program's by a relative error of at most 0.035.
Values may be sent and summed in bfloat16 or wider, within the bound.
A program may use at most 128 MiB of HBM per device.

```python
import jax
import jax.numpy as jnp
from jax import lax

D = 1024
HEADS = 16
KV_HEADS = 8
HEAD_DIM = 128
FF = 3072
LAYERS = 2
SEQ_LEN = 512
TOKENS = 2048


def draw_positions(key, part):
    seq_count = TOKENS // SEQ_LEN
    starts = jax.random.randint(key, (seq_count, SEQ_LEN), 0, 48) == 0
    starts = starts.at[:, 0].set(True)
    starts = starts.at[0, :].set(False)
    starts = starts.at[0, 0].set(True)
    index_row = jnp.arange(SEQ_LEN, dtype=jnp.int32)
    latest = lax.cummax(jnp.where(starts, index_row[None, :], 0), axis=1)
    return (index_row[None, :] - latest).reshape(TOKENS).astype(jnp.int32)


def level_of(own_key, extent, pieces, smallest, high):
    level, own = 1.0, jax.random.fold_in(own_key, 6)
    for dim, parts in pieces:
        steps = jnp.exp(jax.random.uniform(jax.random.fold_in(own, dim), (parts,), jnp.float32, smallest / len(pieces), high / len(pieces)))
        level = level * jnp.repeat(steps, extent[dim] // parts).reshape([-1 if axis == dim else 1 for axis in range(len(extent))])
    return level


def normal_values(rng, extent, spread, limit, pieces=(), kind=jnp.bfloat16):
    loudness = level_of(rng, extent, pieces, -0.22, 0.18) if pieces else 1.0
    values = jax.random.normal(rng, extent, jnp.float32) * spread * loudness
    return jnp.minimum(jnp.maximum(values, -limit), limit).astype(kind)


def setup_inputs(seed: int = 0) -> dict:
    seeds = jax.random.split(jax.random.key(seed), 15)
    return {
        "residual_in": normal_values(seeds[0], (TOKENS, D), 1.0, 6.0, ((0, 4), (1, 8)), jnp.float32),
        "positions": draw_positions(jax.random.fold_in(seeds[14], 71), 0),
        "attn_gain": jnp.clip(1.0 + 0.18 * jax.random.normal(seeds[2], (LAYERS, D), jnp.float32), 0.1, 1.9),
        "query_weight": normal_values(seeds[3], (LAYERS, D, HEADS * HEAD_DIM), D ** -0.5, 0.1875, ((1, 2), (2, 4))),
        "key_weight": normal_values(seeds[4], (LAYERS, D, KV_HEADS * HEAD_DIM), D ** -0.5, 0.1875, ((1, 2), (2, 4))),
        "value_weight": normal_values(seeds[5], (LAYERS, D, KV_HEADS * HEAD_DIM), D ** -0.5, 0.1875, ((1, 2), (2, 4))),
        "query_gain": jnp.clip(1.0 + 0.18 * jax.random.normal(seeds[6], (LAYERS, HEAD_DIM), jnp.float32), 0.1, 1.9),
        "key_gain": jnp.clip(1.0 + 0.18 * jax.random.normal(seeds[7], (LAYERS, HEAD_DIM), jnp.float32), 0.1, 1.9),
        "output_weight": normal_values(seeds[8], (LAYERS, HEADS * HEAD_DIM, D), (HEADS * HEAD_DIM // 64) ** -0.5, 1.0, ((1, 4), (2, 2))),
        "ffn_gain": jnp.clip(1.0 + 0.18 * jax.random.normal(seeds[9], (LAYERS, D), jnp.float32), 0.1, 1.9),
        "gate_weight": normal_values(seeds[10], (LAYERS, D, FF), D ** -0.5, 0.1875, ((1, 2), (2, 4))),
        "up_weight": normal_values(seeds[11], (LAYERS, D, FF), D ** -0.5, 0.1875, ((1, 2), (2, 4))),
        "down_weight": normal_values(seeds[12], (LAYERS, FF, D), FF ** -0.5, 0.109375, ((1, 4), (2, 2))),
        "output_grad": normal_values(seeds[13], (TOKENS, D), 1.0, 6.0, ((0, 4), (1, 8)), jnp.float32),
    }


epsilon = 1e-06
rope_base = 1000000.0
masked_score = -1e+30

def to_bf16(values):
    return lax.optimization_barrier(values.astype(jnp.bfloat16))

def matmul(left, right):
    return jnp.dot(left, right, preferred_element_type=jnp.float32)

def rope_tables(positions):
    halfway = HEAD_DIM // 2
    inverse = rope_base ** (-2.0 * jnp.arange(halfway, dtype=jnp.float32) / HEAD_DIM)
    angles = positions.astype(jnp.float32)[:, None] * inverse[None, :]
    return (jnp.cos(angles), jnp.sin(angles))

def head_prepare(values, gain_vec, cosine, sine):
    scaling = lax.rsqrt(lax.optimization_barrier(jnp.mean(values * values, axis=-1, keepdims=True)) + epsilon)
    normed = values * scaling * gain_vec
    halfway = HEAD_DIM // 2
    front = normed[..., :halfway]
    back_half = normed[..., halfway:]
    cos_b = cosine[:, None, :]
    sin_b = sine[:, None, :]
    return jnp.concatenate([front * cos_b - back_half * sin_b, back_half * cos_b + front * sin_b], axis=-1)

def visible_keys(positions):
    index_row = jnp.arange(positions.shape[0], dtype=jnp.int32)
    offsets = index_row[:, None] - index_row[None, :]
    return (offsets >= 0) & (offsets <= positions[:, None])

def width_norm(residual):
    rate = lax.rsqrt(lax.optimization_barrier(jnp.mean(residual * residual, axis=-1, keepdims=True)) + epsilon)
    return (residual * rate, rate)

def norm_back(grad_feature, normed, rate, gain_vec, grad_res):
    scaled = grad_feature * gain_vec
    inner = lax.optimization_barrier(jnp.mean(scaled * normed, axis=-1, keepdims=True))
    return (grad_res + rate * (scaled - normed * inner), lax.optimization_barrier(jnp.sum(grad_feature * normed, axis=0)))

def attend(query_h, key_h, value_h, allowed):
    group_size = HEADS // KV_HEADS
    key_full = jnp.repeat(key_h, group_size, axis=1).astype(jnp.float32)
    value_full = jnp.repeat(value_h, group_size, axis=1).astype(jnp.float32)
    scores = jnp.einsum('qhd,khd->hqk', query_h.astype(jnp.float32), key_full) * HEAD_DIM ** (-0.5)
    scores = jnp.where(allowed[None], scores, masked_score)
    top_score = lax.optimization_barrier(jnp.max(scores, axis=-1, keepdims=True))
    log_total = top_score + jnp.log(lax.optimization_barrier(jnp.sum(jnp.exp(scores - top_score), axis=-1, keepdims=True)))
    weights = to_bf16(jnp.exp(scores - log_total)).astype(jnp.float32)
    output = jnp.einsum('hqk,khd->qhd', weights, value_full)
    return (to_bf16(output), log_total)

def attend_back(query_h, key_h, value_h, output_h, log_total, grad_out, allowed):
    group_size = HEADS // KV_HEADS
    scale_factor = HEAD_DIM ** (-0.5)
    key_full = jnp.repeat(key_h, group_size, axis=1).astype(jnp.float32)
    value_full = jnp.repeat(value_h, group_size, axis=1).astype(jnp.float32)
    query_f = query_h.astype(jnp.float32)
    scores = jnp.einsum('qhd,khd->hqk', query_f, key_full) * scale_factor
    scores = jnp.where(allowed[None], scores, masked_score)
    prob_values = jnp.exp(scores - log_total)
    weights = to_bf16(prob_values).astype(jnp.float32)
    grad_f = grad_out.astype(jnp.float32)
    row_inner = lax.optimization_barrier(jnp.sum(grad_f * output_h.astype(jnp.float32), axis=-1))
    grad_value = jnp.einsum('hqk,qhd->khd', weights, grad_f)
    grad_weights = jnp.einsum('qhd,khd->hqk', grad_f, value_full)
    grad_scores = to_bf16(prob_values * (grad_weights - row_inner.T[:, :, None])).astype(jnp.float32)
    grad_query = jnp.einsum('hqk,khd->qhd', grad_scores, key_full) * scale_factor
    grad_key = jnp.einsum('hqk,qhd->khd', grad_scores, query_f) * scale_factor
    seq_length = query_h.shape[0]
    grad_key = grad_key.reshape(seq_length, KV_HEADS, group_size, HEAD_DIM).sum(axis=2)
    grad_value = grad_value.reshape(seq_length, KV_HEADS, group_size, HEAD_DIM).sum(axis=2)
    return (grad_query, grad_key, grad_value)

def sequence_pass(params, hidden_in, positions, grad_out):
    attn_gain, query_weight, key_weight, value_weight, query_gain, key_gain, output_weight, ffn_gain, gate_weight, up_weight, down_weight = params
    cosine, sine = rope_tables(positions)
    allowed = visible_keys(positions)
    seq_length = hidden_in.shape[0]
    residual = hidden_in
    saved = []
    for layer_index in range(LAYERS):
        normed_a, rate_a = width_norm(residual)
        feature_a = to_bf16(normed_a * attn_gain[layer_index])
        query_raw = matmul(feature_a, query_weight[layer_index]).reshape(seq_length, HEADS, HEAD_DIM)
        key_raw = matmul(feature_a, key_weight[layer_index]).reshape(seq_length, KV_HEADS, HEAD_DIM)
        value_raw = matmul(feature_a, value_weight[layer_index]).reshape(seq_length, KV_HEADS, HEAD_DIM)
        query_h = to_bf16(head_prepare(query_raw, query_gain[layer_index], cosine, sine))
        key_h = to_bf16(head_prepare(key_raw, key_gain[layer_index], cosine, sine))
        value_h = to_bf16(value_raw)
        attn_out, log_total = attend(query_h, key_h, value_h, allowed)
        mixed_heads = attn_out.reshape(seq_length, HEADS * HEAD_DIM)
        residual_mid = residual + matmul(mixed_heads, output_weight[layer_index])
        normed_f, rate_f = width_norm(residual_mid)
        feature_f = to_bf16(normed_f * ffn_gain[layer_index])
        gate_value = matmul(feature_f, gate_weight[layer_index])
        up_value = matmul(feature_f, up_weight[layer_index])
        sigmoid_gate = jax.nn.sigmoid(gate_value)
        hidden_act = to_bf16(gate_value * sigmoid_gate * up_value)
        saved.append((normed_a, rate_a, feature_a, query_raw, key_raw, query_h, key_h, value_h, attn_out, log_total, mixed_heads, normed_f, rate_f, feature_f, gate_value, up_value, sigmoid_gate, hidden_act))
        residual = residual_mid + matmul(hidden_act, down_weight[layer_index])
    final_out = residual
    grad_res = grad_out
    layer_grads = [None] * LAYERS
    for layer_index in reversed(range(LAYERS)):
        normed_a, rate_a, feature_a, query_raw, key_raw, query_h, key_h, value_h, attn_out, log_total, mixed_heads, normed_f, rate_f, feature_f, gate_value, up_value, sigmoid_gate, hidden_act = saved[layer_index]
        grad_b = to_bf16(grad_res)
        down_grad = matmul(hidden_act.T, grad_b)
        grad_hidden = matmul(grad_b, down_weight[layer_index].T)
        grad_gate = to_bf16(grad_hidden * up_value * sigmoid_gate * (1.0 + gate_value * (1.0 - sigmoid_gate)))
        grad_up = to_bf16(grad_hidden * gate_value * sigmoid_gate)
        gate_grad = matmul(feature_f.T, grad_gate)
        up_grad = matmul(feature_f.T, grad_up)
        grad_feature = matmul(grad_gate, gate_weight[layer_index].T) + matmul(grad_up, up_weight[layer_index].T)
        grad_res, ffn_gain_grad = norm_back(grad_feature, normed_f, rate_f, ffn_gain[layer_index], grad_res)
        grad_b = to_bf16(grad_res)
        output_grad_w = matmul(mixed_heads.T, grad_b)
        grad_mixed = to_bf16(matmul(grad_b, output_weight[layer_index].T)).reshape(seq_length, HEADS, HEAD_DIM)
        grad_query, grad_key, grad_value = attend_back(query_h, key_h, value_h, attn_out, log_total, grad_mixed, allowed)
        unused_q, query_back = jax.vjp(lambda values, gain_vec: head_prepare(values, gain_vec, cosine, sine), query_raw, query_gain[layer_index])
        grad_query_raw, query_gain_part = query_back(grad_query)
        unused_k, key_back = jax.vjp(lambda values, gain_vec: head_prepare(values, gain_vec, cosine, sine), key_raw, key_gain[layer_index])
        grad_key_raw, key_gain_part = key_back(grad_key)
        query_grad_b = to_bf16(grad_query_raw.reshape(seq_length, HEADS * HEAD_DIM))
        key_grad_b = to_bf16(grad_key_raw.reshape(seq_length, KV_HEADS * HEAD_DIM))
        value_grad_b = to_bf16(grad_value.reshape(seq_length, KV_HEADS * HEAD_DIM))
        query_grad_w = matmul(feature_a.T, query_grad_b)
        key_grad_w = matmul(feature_a.T, key_grad_b)
        value_grad_w = matmul(feature_a.T, value_grad_b)
        grad_feature = matmul(query_grad_b, query_weight[layer_index].T) + matmul(key_grad_b, key_weight[layer_index].T) + matmul(value_grad_b, value_weight[layer_index].T)
        grad_res, attn_gain_grad = norm_back(grad_feature, normed_a, rate_a, attn_gain[layer_index], grad_res)
        layer_grads[layer_index] = (attn_gain_grad, query_grad_w, key_grad_w, value_grad_w, query_gain_part, key_gain_part, output_grad_w, ffn_gain_grad, gate_grad, up_grad, down_grad)
    stacked = tuple((jnp.stack([layer_grads[index][member] for index in range(LAYERS)]) for member in range(11)))
    return (final_out, grad_res, stacked)

def reference(residual_in, positions, attn_gain, query_weight, key_weight, value_weight, query_gain, key_gain, output_weight, ffn_gain, gate_weight, up_weight, down_weight, output_grad):
    params = (attn_gain, query_weight, key_weight, value_weight, query_gain, key_gain, output_weight, ffn_gain, gate_weight, up_weight, down_weight)
    seq_count = residual_in.shape[0] // SEQ_LEN
    stacked_in = residual_in.reshape(seq_count, SEQ_LEN, D)
    stacked_pos = positions.reshape(seq_count, SEQ_LEN)
    stacked_grad = output_grad.reshape(seq_count, SEQ_LEN, D)
    zeros_init = tuple((jnp.zeros(param.shape, jnp.float32) for param in params))

    def scan_step(carry, inputs):
        final_out, grad_in, grads = sequence_pass(params, inputs[0], inputs[1], inputs[2])
        return (tuple((left + right for left, right in zip(carry, grads))), (final_out, grad_in))
    totals, (outputs, input_grads) = lax.scan(scan_step, zeros_init, (stacked_in, stacked_pos, stacked_grad))
    return (outputs.reshape(residual_in.shape[0], D), input_grads.reshape(residual_in.shape[0], D), totals[0], totals[1], totals[2], totals[3], totals[4], totals[5], totals[6], totals[7], totals[8], totals[9], totals[10])
```

```python
import functools
import math

import jax
import jax.numpy as jnp
from jax import lax
from jax.experimental import pallas as pl
from jax.experimental.pallas import tpu as pltpu
from jax.sharding import PartitionSpec as P

HEAD_DIM = 128
SEQ_LEN = 512

epsilon = 1e-06
rope_base = 1000000.0
masked_score = -1e30
MESH = pl.DeviceIdType.MESH
BF = jnp.bfloat16
F32 = jnp.float32
SCALE = HEAD_DIM ** (-0.5)
LOG2E = math.log2(math.e)
VM = pl.BlockSpec(memory_space=pltpu.VMEM)
ANY = pl.BlockSpec(memory_space=pl.ANY)


def dot(left, right, dims):
    return lax.dot_general(left, right, (dims, ((), ())), preferred_element_type=F32)


def mm(left, right):
    return dot(left, right, ((1,), (0,)))


def mm_t(left, right):
    return dot(left, right, ((1,), (1,)))


def t_mm(left, right):
    return dot(left, right, ((0,), (0,)))


def at(index, size):
    return pl.ds(pl.multiple_of(index * size, size), size)


def half_turn(values):
    return pltpu.roll(values, HEAD_DIM // 2, 1)


def head_norm(values):
    scaling = lax.rsqrt(jnp.mean(values * values, axis=-1, keepdims=True) + epsilon)
    return values * scaling, scaling


def head_prepare(values, gain, cosine, sine):
    normed = head_norm(values)[0] * gain
    return (normed * cosine + half_turn(normed) * sine).astype(BF)


def head_back(grad, values, gain, cosine, sine):
    normed, scaling = head_norm(values)
    turned = grad * cosine + half_turn(grad * sine)
    scaled = turned * gain
    inner = jnp.mean(scaled * normed, axis=-1, keepdims=True)
    return (
        scaling * (scaled - normed * inner),
        jnp.sum(turned * normed, axis=0, keepdims=True),
    )


def width_norm(residual):
    rate = lax.rsqrt(jnp.mean(residual * residual, axis=1, keepdims=True) + epsilon)
    return residual * rate, rate


class Net:
    def __init__(self, send, recv, limit):
        self.send, self.recv, self.limit, self.used = send, recv, limit, 0

    def copy(self, source, target, device):
        index = self.used
        self.used += 1
        assert index < self.limit
        made = pltpu.make_async_remote_copy(
            src_ref=source,
            dst_ref=target,
            send_sem=self.send.at[index],
            recv_sem=self.recv.at[index],
            device_id=device,
            device_id_type=MESH,
        )
        made.start()
        return made


def layers_kernel(sizes, shapes):
    dp, rows, cols = sizes
    group = rows * cols
    layers, tokens, block, head_cols, kv_cols, ff = shapes
    width = block * group
    slab = width // rows
    size = tokens // group
    q_heads, kv_heads = head_cols // HEAD_DIM, kv_cols // HEAD_DIM
    members = q_heads // kv_heads
    qkv_cols = head_cols + 2 * kv_cols
    q_block = min(SEQ_LEN, 256)
    limit = 256
    chip = rows * size

    pieces = []
    for layer in reversed(range(layers)):
        pieces.append(("down", layer, 0, rows * ff))
        for part in range(2):
            pieces.append(("gu", layer, part * slab // 2, slab // 2))
        pieces.append(("o", layer, 0, rows * head_cols))
        for part in range(2):
            pieces.append(("qkv", layer, part * slab // 2, slab // 2))
    n_pieces = len(pieces)

    grad_shapes = {
        "down": (layers, rows * ff, slab),
        "gu": (layers, slab, 2 * rows * ff),
        "o": (layers, rows * head_cols, slab),
        "qkv": (layers, slab, rows * qkv_cols),
    }
    grad_names = list(grad_shapes)

    scratch = {
        "x0": ((group, tokens + 16, block), BF),
        "t0": ((group, tokens, block), BF),
        "fin": ((size, width), F32),
        "gains": ((8, width), F32),
        "mask": ((tokens, SEQ_LEN), F32),
        "wqkv": ((layers, width, qkv_cols), BF),
        "wo": ((layers, head_cols, width), BF),
        "wgu": ((layers, width, 2 * ff), BF),
        "wd": ((layers, ff, width), BF),
        "feat_a": ((layers, tokens, width), BF),
        "feat_f": ((layers, tokens, width), BF),
        "res": ((2 * layers, size, width), F32),
        "raw": ((layers, tokens, qkv_cols), F32),
        "prep": ((layers, tokens, qkv_cols), BF),
        "inv": ((tokens, HEAD_DIM), F32),
        "att": ((layers, rows, tokens, head_cols), BF),
        "gu": ((layers, tokens, 2 * ff), F32),
        "hid": ((layers, rows, tokens, ff), BF),
        "part": ((tokens, width), BF),
        "got_row": ((2, max(rows - 1, 1), cols, size, width), BF),
        "mid": ((max(cols - 1, 1), size, width), BF),
        "got_col": ((2, max(cols - 1, 1), size, width), BF),
        "gb": ((2, tokens, width), BF),
        "dgu": ((rows, tokens, 2 * ff), BF),
        "dqkv": ((rows, tokens, qkv_cols), BF),
        "datt": ((tokens, head_cols), BF),
        "dkv": ((2, tokens, HEAD_DIM), F32),
        "dq": ((tokens, HEAD_DIM), F32),
        "gtok": ((size, width), F32),
        "sums": ((group, 16, HEAD_DIM), F32),
        "sums_in": ((group, 16, HEAD_DIM), F32),
        "dsum": ((dp, 16, HEAD_DIM), F32),
    }
    for name in grad_names:
        scratch["acc_" + name] = (grad_shapes[name], BF)
        scratch["frm_" + name] = (grad_shapes[name], BF)
    names = list(scratch)

    def kernel(
        x_ref, og_ref, gain_ref, hg_ref, cos_ref, sin_ref, pos_ref,
        wq_ref, wk_ref, wv_ref, wo_ref, wg_ref, wu_ref, wd_ref,
        out_ref, din_ref, small_ref, t_down, t_gu, t_o, t_qkv, *rest,
    ):
        ref = dict(zip(names, rest))
        send, recv, local, up_send, up_recv, in_send, in_recv = rest[len(names):]
        totals = dict(zip(grad_names, (t_down, t_gu, t_o, t_qkv)))
        net = Net(send, recv, limit)
        row, col, place = lax.axis_index("row"), lax.axis_index("col"), lax.axis_index("dp")
        me = row * cols + col
        row_peers = [lax.rem(row + step, rows) for step in range(1, rows)]
        col_peers = [lax.rem(col + step, cols) for step in range(1, cols)]
        others = [
            (lax.rem(row + down, rows), lax.rem(col + over, cols))
            for down in range(rows)
            for over in range(cols)
            if down or over
        ]

        staged = []
        counter = [0]

        def weight_moves(layer):
            return [
                (wq_ref, "wqkv", 1, head_cols, 0),
                (wk_ref, "wqkv", 1, kv_cols, head_cols),
                (wv_ref, "wqkv", 1, kv_cols, head_cols + kv_cols),
                (wo_ref, "wo", 0, head_cols, 0),
                (wg_ref, "wgu", 1, ff, 0),
                (wu_ref, "wgu", 1, ff, ff),
                (wd_ref, "wd", 0, ff, 0),
            ]

        def weight_pair(move, layer, owner):
            source, name, split, extent, start = move
            if split == 1:
                return (
                    source.at[layer, :, at(owner, extent)],
                    ref[name].at[layer, at(row, slab), pl.ds(start, extent)],
                )
            return (
                source.at[layer, at(owner, extent), :],
                ref[name].at[layer, :, at(row, slab)],
            )

        own_weights = {}
        for layer in range(layers):
            for move in weight_moves(layer):
                source, target = weight_pair(move, layer, row)
                copy = pltpu.make_async_copy(source, target, local.at[counter[0]])
                copy.start()
                counter[0] += 1
                own_weights.setdefault((layer, move[1]), []).append(copy)

        x0 = ref["x0"]
        gain = gain_ref[...]
        high = gain.astype(BF)
        middle = (gain - high.astype(F32)).astype(BF)
        low = (gain - high.astype(F32) - middle.astype(F32)).astype(BF)
        zeros = jnp.zeros((16 - 3 * 2 * layers, block), BF)
        count = 2 * layers
        x0[me, pl.ds(0, tokens), :] = x_ref[...].astype(BF)
        x0[me, pl.ds(tokens, 16), :] = jnp.concatenate(
            [high[:count].astype(F32), middle[:count].astype(F32), low[:count].astype(F32),
             zeros.astype(F32)], axis=0
        ).astype(BF)

        barrier = pltpu.get_barrier_semaphore()
        greeted = [{"row": there[0], "col": there[1]} for there in others]
        greeted += [{"dp": lax.rem(place + step, dp)} for step in range(1, dp)]
        for peer in greeted:
            pl.semaphore_signal(barrier, inc=1, device_id=peer, device_id_type=MESH)
        pl.semaphore_wait(barrier, len(greeted))

        def gather_start(view):
            mine = view(row, col)
            over = [None] * cols
            for step in range(cols - 1, 0, -1):
                over[step] = net.copy(mine, mine, {"col": col_peers[step - 1]})
            down = [[net.copy(mine, mine, {"row": peer}) for peer in row_peers]]
            return view, over, down

        def gather_step(state, step):
            view, over, down = state
            if step:
                over[step].wait_recv()
                here = view(row, lax.rem(col + cols - step, cols))
                down.append([net.copy(here, here, {"row": peer}) for peer in row_peers])

        def gather_rows(state, step):
            for copy in state[2][step]:
                copy.wait_recv()

        def gather_end(state):
            for copy in state[1][1:]:
                copy.wait_send()
            for line in state[2]:
                for copy in line:
                    copy.wait_send()

        def gather_rest(state):
            for step in range(1, cols):
                gather_step(state, step)
            for step in range(cols):
                gather_rows(state, step)
            gather_end(state)

        def chip_rows(source, target):
            parts = [source[at(there * cols + target, size), :] for there in range(rows)]
            return jnp.concatenate(parts, axis=0) if rows > 1 else parts[0]

        def store_rows(target_ref, target, value):
            for there in range(rows):
                target_ref[at(there * cols + target, size), :] = value[
                    there * size : (there + 1) * size
                ]

        part, mid = ref["part"], ref["mid"]

        def scatter(compute, order, fill_a=None, gather=None, slots=0):
            first, second = {}, {}
            got_row, got_col = ref["got_row"].at[slots], ref["got_col"].at[slots]

            def pair_sum(step):
                target = lax.rem(col + cols - step, cols)
                total = part[at(row * cols + target, size), :].astype(F32)
                for slot in range(rows - 1):
                    first[slot, step].wait_recv()
                    total += got_row[slot, step].astype(F32)
                return total

            def forward(step):
                mid[step - 1] = pair_sum(step).astype(BF)
                target = lax.rem(col + cols - step, cols)
                second[step] = net.copy(mid.at[step - 1], got_col.at[step - 1], {"col": target})

            waiting = []
            for step in order:
                target = lax.rem(col + cols - step, cols)
                if gather is not None:
                    gather_step(gather, step)
                    gather_rows(gather, step)
                store_rows(part, target, compute(target).astype(BF))
                for slot, peer in enumerate(row_peers):
                    first[slot, step] = net.copy(
                        part.at[at(peer * cols + target, size), :],
                        got_row.at[slot, step],
                        {"row": peer},
                    )
                if waiting:
                    forward(waiting.pop())
                if step:
                    waiting.append(step)
            for step in waiting:
                forward(step)
            if gather is not None:
                gather_end(gather)
            if fill_a is not None:
                fill_a()
            total = pair_sum(0)
            for step in range(1, cols):
                second[step].wait_recv()
                total += got_col[step - 1].astype(F32)
            for copy in list(first.values()) + list(second.values()):
                copy.wait_send()
            return total

        late = list(range(1, cols)) + [0]
        early = list(range(cols))

        def feature_view(buffer):
            return lambda at_row, at_col: buffer.at[at_row * cols + at_col]

        def token_view(buffer):
            return lambda at_row, at_col: buffer.at[at(at_row * cols + at_col, size), :]

        first_gather = gather_start(feature_view(x0))

        sent_weights = {}

        def send_weights(layer):
            for move in weight_moves(layer):
                for peer in row_peers:
                    source, target = weight_pair(move, layer, peer)
                    sent_weights.setdefault((layer, move[1]), []).append(
                        net.copy(source, target, {"row": peer})
                    )

        def need_weight(layer, name):
            for copy in own_weights.pop((layer, name), []):
                copy.wait()
            for copy in sent_weights.pop((layer, name), []):
                copy.wait()

        def to_tokens(source, target):
            copies = []
            for there in others:
                index = there[0] * cols + there[1]
                copies.append(
                    net.copy(
                        source.at[at(index, size), :],
                        target.at[:, at(me, block)],
                        {"row": there[0], "col": there[1]},
                    )
                )
            target[:, at(me, block)] = source[at(me, size), :]
            return copies

        def to_features(source, target):
            copies = []
            for there in others:
                index = there[0] * cols + there[1]
                copies.append(
                    net.copy(
                        source.at[:, at(index, block)],
                        target.at[at(me, size), :],
                        {"row": there[0], "col": there[1]},
                    )
                )
            target[at(me, size), :] = source[:, at(me, block)]
            return copies

        send_weights(0)

        for start in range(0, tokens, SEQ_LEN):
            shape = (SEQ_LEN, SEQ_LEN)
            offset = lax.broadcasted_iota(jnp.int32, shape, 0) - lax.broadcasted_iota(
                jnp.int32, shape, 1
            )
            seen = (offset >= 0) & (offset <= pos_ref[pl.ds(start, SEQ_LEN), :])
            ref["mask"][pl.ds(start, SEQ_LEN), :] = jnp.where(seen, 0.0, masked_score)

        gather_rest(first_gather)
        residual_moves = to_tokens(x_ref, ref["res"].at[0])

        gains = ref["gains"]
        for slot in range(group):
            split = x0[slot, pl.ds(tokens, 16), :].astype(F32)
            gains[0:count, slot * block : (slot + 1) * block] = (
                split[:count] + split[count : 2 * count] + split[2 * count : 3 * count]
            )

        for start in range(0, tokens, 128):
            length = pl.ds(start, 128)
            squares = jnp.zeros((128, block), F32)
            for slot in range(group):
                value = x0[slot, length, :].astype(F32)
                squares += value * value
            rate = lax.rsqrt(jnp.sum(squares, axis=1, keepdims=True) * (1.0 / width) + epsilon)
            for slot in range(group):
                lanes = slice(slot * block, (slot + 1) * block)
                ref["feat_a"][0, length, lanes] = (
                    x0[slot, length, :].astype(F32) * rate * gains[0:1, lanes]
                ).astype(BF)

        state = {}

        def attend(layer):
            raw, prep, att = (ref[k].at[layer] for k in ("raw", "prep", "att"))
            inv = ref["inv"]
            gain_q, gain_k = hg_ref[2 * layer : 2 * layer + 1], hg_ref[2 * layer + 1 : 2 * layer + 2]
            cosine, sine = cos_ref[...], sin_ref[...]
            for head in range(q_heads + kv_heads):
                lanes = slice(head * HEAD_DIM, (head + 1) * HEAD_DIM)
                gain_h = gain_q if head < q_heads else gain_k
                prep[:, lanes] = head_prepare(raw[:, lanes], gain_h, cosine, sine)
            prep[:, head_cols + kv_cols :] = raw[:, head_cols + kv_cols :].astype(BF)
            for start in range(0, tokens, SEQ_LEN):
                for head in range(q_heads):
                    kv = head // members
                    k_lanes = slice(head_cols + kv * HEAD_DIM, head_cols + (kv + 1) * HEAD_DIM)
                    v_at = head_cols + kv_cols + kv * HEAD_DIM
                    v_lanes = slice(v_at, v_at + HEAD_DIM)
                    lanes = slice(head * HEAD_DIM, (head + 1) * HEAD_DIM)
                    for begin in range(0, SEQ_LEN, q_block):
                        mine = pl.ds(start + begin, q_block)
                        keys = pl.ds(start, begin + q_block)
                        scores = mm_t(prep[mine, lanes], prep[keys, k_lanes])
                        weights = jnp.exp2(
                            scores * (SCALE * LOG2E)
                            + ref["mask"][mine, 0 : begin + q_block]
                        )
                        inverse = 1.0 / jnp.sum(weights, axis=-1, keepdims=True)
                        lane = layer * q_heads + head
                        inv[mine, lane : lane + 1] = inverse
                        att[row, mine, lanes] = mm(
                            (weights * inverse).astype(BF), prep[keys, v_lanes]
                        ).astype(BF)

        def feature_block(value, gain_row, target):
            normed, rate = width_norm(value)
            target[at(me, size), :] = (normed * gains[gain_row : gain_row + 1, :]).astype(BF)

        def send_row(buffer):
            return [net.copy(buffer.at[row], buffer.at[row], {"row": peer}) for peer in row_peers]

        row_moves = {}
        for layer in range(layers):
            feat_a, feat_f = ref["feat_a"].at[layer], ref["feat_f"].at[layer]
            raw = ref["raw"].at[layer]
            need_weight(layer, "wqkv")
            for start in range(0, qkv_cols, 256):
                lanes = slice(start, min(start + 256, qkv_cols))
                raw[:, lanes] = mm(feat_a[...], ref["wqkv"][layer, :, lanes])
            if layer == 0:
                for extra in range(1, layers):
                    send_weights(extra)
                ref["t0"][me] = og_ref[...].astype(BF)
                top_gather = gather_start(feature_view(ref["t0"]))
                grad_moves = to_tokens(og_ref, ref["gtok"])
            attend(layer)
            row_moves["att", layer] = send_row(ref["att"].at[layer])
            need_weight(layer, "wo")

            def compute_o(target, layer=layer):
                return mm(chip_rows(ref["att"].at[layer, row], target), ref["wo"][layer])

            if layer == 0:
                gather_rest(top_gather)
            total = scatter(compute_o, late)
            if layer == 0:
                for copy in residual_moves:
                    copy.wait()
            ref["res"][2 * layer + 1] = ref["res"][2 * layer] + total
            feature_block(ref["res"][2 * layer + 1], layers + layer, feat_f)
            gathering = gather_start(token_view(feat_f))
            need_weight(layer, "wgu")
            need_weight(layer, "wd")

            def compute_ff(target, layer=layer):
                feat = chip_rows(ref["feat_f"].at[layer], target)
                both = mm(feat, ref["wgu"][layer])
                store_rows(ref["gu"].at[layer], target, both)
                gate, up = both[:, :ff], both[:, ff:]
                hidden = (gate * lax.logistic(gate) * up).astype(BF)
                store_rows(ref["hid"].at[layer, row], target, hidden)
                return mm(hidden, ref["wd"][layer])

            total = scatter(compute_ff, early, gather=gathering)
            row_moves["hid", layer] = send_row(ref["hid"].at[layer])
            result = ref["res"][2 * layer + 1] + total
            if layer < layers - 1:
                ref["res"][2 * layer + 2] = result
                feature_block(result, layer + 1, ref["feat_a"].at[layer + 1])
                gather_rest(gather_start(token_view(ref["feat_a"].at[layer + 1])))
            else:
                ref["fin"][...] = result
                out_moves = to_features(ref["fin"], out_ref)

        half = dp // 2
        on_left = place < half
        depth = jnp.where(on_left, place, dp - 1 - place)
        inward = jnp.where(on_left, place + 1, place - 1)
        outward = jnp.where(on_left, place - 1, place + 1)
        outward = jnp.clip(outward, 0, dp - 1)
        is_mid = depth == half - 1
        inner = depth > 0

        def views(index):
            name, layer, start, extent = pieces[index]
            rows_at = pl.ds(start, extent)
            return (
                ref["acc_" + name].at[layer, rows_at, :],
                ref["frm_" + name].at[layer, rows_at, :],
                totals[name].at[layer, rows_at, :],
            )

        def hop(source, target, index, kind, peer):
            sems = {
                "up": (up_send, up_recv),
                "across": (up_send, in_recv),
                "back": (in_send, in_recv),
            }[kind]
            return pltpu.make_async_remote_copy(
                src_ref=source,
                dst_ref=target,
                send_sem=sems[0].at[index],
                recv_sem=sems[1].at[index],
                device_id={"dp": peer},
                device_id_type=MESH,
            )

        def send_inward(index, condition):
            acc, frm, tot = views(index)

            @pl.when(condition & jnp.logical_not(is_mid))
            def _():
                hop(acc, frm, index, "up", inward).start()

            @pl.when(condition & is_mid)
            def _():
                hop(acc, tot, index, "across", inward).start()

        def add_into(target, one, two):
            extent = one.shape[0]
            chunk = 32

            def body(step, carry):
                here = at(step, chunk)
                target[here, :] = (one[here, :].astype(F32) + two[here, :].astype(F32)).astype(BF)
                return carry

            lax.fori_loop(0, extent // chunk, body, 0)

        def stage(index, number):
            acc, frm, tot = views(index)
            if number == 0:
                send_inward(index, jnp.logical_not(inner))
            if number == 1:
                @pl.when(inner)
                def _():
                    hop(acc, frm, index, "up", inward).wait_recv()
                    add_into(acc, acc, frm)

                send_inward(index, inner)
            if number == 2:
                @pl.when(is_mid)
                def _():
                    hop(acc, tot, index, "across", inward).wait_recv()
                    add_into(tot, acc, tot)

                @pl.when(is_mid & inner)
                def _():
                    hop(tot, tot, index, "back", outward).start()
            if number == 3:
                @pl.when(jnp.logical_not(is_mid))
                def _():
                    hop(tot, tot, index, "back", inward).wait_recv()

                @pl.when(jnp.logical_not(is_mid) & inner)
                def _():
                    hop(tot, tot, index, "back", outward).start()

        done = {"next": 0, "up": 0, "across": 0, "back": 0}

        def launch(count_new):
            for _ in range(count_new):
                stage(done["next"], 0)
                done["next"] += 1

        def pump(lag):
            if done["up"] < done["next"] - lag:
                stage(done["up"], 1)
                done["up"] += 1
            if done["across"] < done["up"] - 1:
                stage(done["across"], 2)
                done["across"] += 1

        def finish():
            while done["back"] < n_pieces:
                if done["up"] < n_pieces:
                    stage(done["up"], 1)
                    done["up"] += 1
                if done["across"] < done["up"] - 1 or done["up"] == n_pieces and done["across"] < n_pieces:
                    stage(done["across"], 2)
                    done["across"] += 1
                if done["back"] < done["across"] - 1 or done["across"] == n_pieces:
                    stage(done["back"], 3)
                    done["back"] += 1
            for index in range(n_pieces):
                acc, frm, tot = views(index)
                hop(acc, frm, index, "up", inward).wait_send()

                @pl.when(inner)
                def _(index=index, tot=tot):
                    hop(tot, tot, index, "back", outward).wait_send()

        gb, gb2 = ref["gb"].at[0], ref["gb"].at[1]
        for slot in range(group):
            gb[:, slot * block : (slot + 1) * block] = ref["t0"][slot]
        for copy in grad_moves:
            copy.wait()
        gtok, sums = ref["gtok"], ref["sums"]
        for slot in range(group):
            sums[slot] = jnp.zeros((16, HEAD_DIM), F32)

        def slab_of(source):
            return source[:, at(row, slab)]

        def norm_back(total, residual, gain_row):
            normed, rate = width_norm(residual)
            scaled = total * gains[gain_row : gain_row + 1, :]
            inner_mean = jnp.mean(scaled * normed, axis=1, keepdims=True)
            gtok[...] = gtok[...] + rate * (scaled - normed * inner_mean)
            line = jnp.sum(total * normed, axis=0, keepdims=True)
            for slot in range(group):
                sums[slot, gain_row : gain_row + 1, :] = line[:, slot * block : (slot + 1) * block]

        def attend_back(layer):
            raw, prep, att = (ref[k].at[layer] for k in ("raw", "prep", "att"))
            inv = ref["inv"]
            gain_q, gain_k = hg_ref[2 * layer : 2 * layer + 1], hg_ref[2 * layer + 1 : 2 * layer + 2]
            dqkv, datt = ref["dqkv"], ref["datt"]
            dk, dv, dq = ref["dkv"].at[0], ref["dkv"].at[1], ref["dq"]
            cosine, sine = cos_ref[...], sin_ref[...]
            total_q = jnp.zeros((1, HEAD_DIM), F32)
            total_k = jnp.zeros((1, HEAD_DIM), F32)
            for kv in range(kv_heads):
                k_lanes = slice(head_cols + kv * HEAD_DIM, head_cols + (kv + 1) * HEAD_DIM)
                v_at = head_cols + kv_cols + kv * HEAD_DIM
                v_lanes = slice(v_at, v_at + HEAD_DIM)
                dk[...] = jnp.zeros((tokens, HEAD_DIM), F32)
                dv[...] = jnp.zeros((tokens, HEAD_DIM), F32)
                for member in range(members):
                    head = kv * members + member
                    lanes = slice(head * HEAD_DIM, (head + 1) * HEAD_DIM)
                    lane = layer * q_heads + head
                    for start in range(0, tokens, SEQ_LEN):
                        for begin in range(0, SEQ_LEN, q_block):
                            mine = pl.ds(start + begin, q_block)
                            keys = pl.ds(start, begin + q_block)
                            scores = mm_t(prep[mine, lanes], prep[keys, k_lanes])
                            probs = jnp.exp2(
                                scores * (SCALE * LOG2E)
                                + ref["mask"][mine, 0 : begin + q_block]
                            ) * inv[mine, lane : lane + 1]
                            grad_o = datt[mine, lanes]
                            inner_sum = jnp.sum(
                                grad_o.astype(F32) * att[row, mine, lanes].astype(F32),
                                axis=-1,
                                keepdims=True,
                            )
                            dv[keys, :] += t_mm(probs.astype(BF), grad_o)
                            grad_s = (
                                probs * (mm_t(grad_o, prep[keys, v_lanes]) - inner_sum)
                            ).astype(BF)
                            dq[mine, :] = mm(grad_s, prep[keys, k_lanes]) * SCALE
                            dk[keys, :] += t_mm(grad_s, prep[mine, lanes])
                    back, line = head_back(dq[...], raw[:, lanes], gain_q, cosine, sine)
                    dqkv[row, :, lanes] = back.astype(BF)
                    total_q += line
                back, line = head_back(dk[...] * SCALE, raw[:, k_lanes], gain_k, cosine, sine)
                dqkv[row, :, k_lanes] = back.astype(BF)
                dqkv[row, :, v_lanes] = dv[...].astype(BF)
                total_k += line
            at_row = 8 + 2 * layer
            for slot in range(group):
                sums[slot, at_row : at_row + 1, :] = total_q
                sums[slot, at_row + 1 : at_row + 2, :] = total_k

        for layer in reversed(range(layers)):
            feat_a, feat_f = ref["feat_a"].at[layer], ref["feat_f"].at[layer]
            if layer == layers - 1:
                gathering = None
            else:
                gb[at(me, size), :] = gtok[...].astype(BF)
                gathering = gather_start(token_view(gb))

            def compute_ff_back(target, layer=layer):
                grad = chip_rows(gb, target)
                both = chip_rows(ref["gu"].at[layer], target)
                gate, up = both[:, :ff], both[:, ff:]
                dhid = mm_t(grad, ref["wd"][layer])
                sig = lax.logistic(gate)
                dgate = (dhid * up * sig * (1.0 + gate * (1.0 - sig))).astype(BF)
                dup = (dhid * gate * sig).astype(BF)
                joined = jnp.concatenate([dgate, dup], axis=1)
                store_rows(ref["dgu"].at[row], target, joined)
                return mm_t(joined, ref["wgu"][layer])

            def ffn_grads(layer=layer, feat_f=feat_f):
                for copy in row_moves.pop(("hid", layer)):
                    copy.wait()
                moves = send_row(ref["dgu"])
                right = slab_of(gb)
                for there in range(rows):
                    ref["acc_down"][layer, there * ff : (there + 1) * ff, :] = t_mm(
                        ref["hid"][layer, there], right
                    ).astype(BF)
                launch(1)
                for copy in moves:
                    copy.wait()
                left = slab_of(feat_f)
                for there in range(rows):
                    value = t_mm(left, ref["dgu"][there]).astype(BF)
                    ref["acc_gu"][layer, :, there * ff : (there + 1) * ff] = value[:, :ff]
                    begin = (rows + there) * ff
                    ref["acc_gu"][layer, :, begin : begin + ff] = value[:, ff:]
                launch(2)
                pump(2)

            total = scatter(
                compute_ff_back, late if gathering is None else early,
                fill_a=ffn_grads, gather=gathering, slots=int(gathering is None),
            )
            norm_back(total, ref["res"][2 * layer + 1], layers + layer)
            gb2[at(me, size), :] = gtok[...].astype(BF)
            gathering = gather_start(token_view(gb2))
            pump(2)
            gather_rest(gathering)
            for start in range(0, tokens, 256):
                ref["datt"][start : start + 256, :] = mm_t(
                    gb2[start : start + 256, :], ref["wo"][layer]
                ).astype(BF)
            attend_back(layer)
            moves = send_row(ref["dqkv"])

            def compute_qkv_back(target, layer=layer):
                return mm_t(chip_rows(ref["dqkv"].at[row], target), ref["wqkv"][layer])

            def attn_grads(layer=layer, feat_a=feat_a, moves=moves):
                for copy in row_moves.pop(("att", layer)):
                    copy.wait()
                right = slab_of(gb2)
                for there in range(rows):
                    ref["acc_o"][layer, there * head_cols : (there + 1) * head_cols, :] = t_mm(
                        ref["att"][layer, there], right
                    ).astype(BF)
                launch(1)
                for copy in moves:
                    copy.wait()
                left = slab_of(feat_a)
                for there in range(rows):
                    value = t_mm(left, ref["dqkv"][there]).astype(BF)
                    acc = ref["acc_qkv"]
                    acc[layer, :, there * head_cols : (there + 1) * head_cols] = value[:, :head_cols]
                    begin = rows * head_cols + there * kv_cols
                    acc[layer, :, begin : begin + kv_cols] = value[
                        :, head_cols : head_cols + kv_cols
                    ]
                    begin += rows * kv_cols
                    acc[layer, :, begin : begin + kv_cols] = value[:, head_cols + kv_cols :]
                launch(2)
                pump(2)

            total = scatter(compute_qkv_back, late, fill_a=attn_grads)
            norm_back(total, ref["res"][2 * layer], layer)

        for copy in out_moves:
            copy.wait()
        sums_in, dsum = ref["sums_in"], ref["dsum"]
        sum_moves = []
        for there in others:
            index = there[0] * cols + there[1]
            sum_moves.append(
                net.copy(sums.at[index], sums_in.at[me], {"row": there[0], "col": there[1]})
            )
        sums_in[me] = sums[me]
        din_moves = to_features(gtok, din_ref)
        for copy in sum_moves:
            copy.wait()
        total = sums_in[0]
        for slot in range(1, group):
            total += sums_in[slot]
        dsum[place] = total
        sum_moves = [
            net.copy(dsum.at[place], dsum.at[place], {"dp": lax.rem(place + step, dp)})
            for step in range(1, dp)
        ]
        for copy in din_moves:
            copy.wait()
        for copy in sum_moves:
            copy.wait()
        total = dsum[0]
        for slot in range(1, dp):
            total += dsum[slot]
        small_ref[...] = total
        finish()

    def call(*operands):
        shapes_out = [
            jax.ShapeDtypeStruct((tokens, block), F32),
            jax.ShapeDtypeStruct((tokens, block), F32),
            jax.ShapeDtypeStruct((16, HEAD_DIM), F32),
        ] + [jax.ShapeDtypeStruct(grad_shapes[name], BF) for name in grad_names]
        return pl.pallas_call(
            kernel,
            name="layers",
            out_shape=shapes_out,
            in_specs=[VM] * 7 + [ANY] * 7,
            out_specs=[VM] * len(shapes_out),
            scratch_shapes=[pltpu.VMEM(*scratch[name]) for name in names]
            + [
                pltpu.SemaphoreType.DMA((limit,)),
                pltpu.SemaphoreType.DMA((limit,)),
                pltpu.SemaphoreType.DMA((7 * layers,)),
            ]
            + [pltpu.SemaphoreType.DMA((n_pieces,))] * 4,
            compiler_params=pltpu.CompilerParams(
                collective_id=1, has_side_effects=True, vmem_limit_bytes=60 << 20
            ),
        )(*operands)

    return call


def per_device(
    sizes,
    residual_in,
    positions,
    attn_gain,
    query_weight,
    key_weight,
    value_weight,
    query_gain,
    key_gain,
    output_weight,
    ffn_gain,
    gate_weight,
    up_weight,
    down_weight,
    output_grad,
):
    dp, rows, cols = sizes
    layers = query_weight.shape[0]
    tokens, block = residual_in.shape
    halfway = HEAD_DIM // 2
    inverse = rope_base ** (-2.0 * jnp.arange(halfway, dtype=F32) / HEAD_DIM)
    angles = positions.astype(F32)[:, None] * inverse[None, :]
    cosine, sine = jnp.cos(angles), jnp.sin(angles)
    cosine = jnp.concatenate([cosine, cosine], axis=1)
    sine = jnp.concatenate([-sine, sine], axis=1)

    gains = jnp.concatenate([attn_gain, ffn_gain])
    head_gains = jnp.stack([query_gain, key_gain], axis=1).reshape(2 * layers, HEAD_DIM)
    shapes = (
        layers, tokens, block, query_weight.shape[2] // rows, key_weight.shape[2] // rows,
        gate_weight.shape[2] // rows,
    )
    outputs, input_grad, small, down, gu, out_w, qkv = layers_kernel(sizes, shapes)(
        residual_in, output_grad, gains, head_gains, cosine, sine, positions[:, None],
        query_weight, key_weight, value_weight, output_weight, gate_weight, up_weight, down_weight,
    )
    wide_q, wide_k, wide_f = query_weight.shape[2], key_weight.shape[2], gate_weight.shape[2]
    head_sum = small[8 : 8 + 2 * layers].reshape(layers, 2, HEAD_DIM)
    return (
        outputs,
        input_grad,
        small[:layers],
        qkv[:, :, :wide_q].astype(F32),
        qkv[:, :, wide_q : wide_q + wide_k].astype(F32),
        qkv[:, :, wide_q + wide_k :].astype(F32),
        head_sum[:, 0],
        head_sum[:, 1],
        out_w.astype(F32),
        small[layers : 2 * layers],
        gu[:, :, :wide_f].astype(F32),
        gu[:, :, wide_f:].astype(F32),
        down.astype(F32),
    )


def solution(mesh):
    wide = P("dp", ("row", "col"))
    gain = P(None, ("row", "col"))
    into, out_of = P(None, "row", "col"), P(None, "col", "row")
    in_specs = (
        wide, P("dp"), gain, into, into, into, P(), P(), out_of, gain, into, into, out_of, wide,
    )
    out_specs = (wide, wide, gain, into, into, into, P(), P(), out_of, gain, into, into, out_of)
    return jax.shard_map(
        functools.partial(per_device, (mesh.shape["dp"], mesh.shape["row"], mesh.shape["col"])),
        mesh=mesh,
        in_specs=in_specs,
        out_specs=out_specs,
        check_vma=False,
    )
```

```python
import functools
import math

import jax
import jax.numpy as jnp
from jax import lax
from jax.experimental import pallas as pl
from jax.experimental.pallas import tpu as pltpu
from jax.sharding import PartitionSpec as P

HEAD_DIM = 128
SEQ_LEN = 512

epsilon = 1e-06
rope_base = 1000000.0
masked_score = -1e30
MESH = pl.DeviceIdType.MESH
BF = jnp.bfloat16
F32 = jnp.float32
SCALE = HEAD_DIM ** (-0.5)
LOG2E = math.log2(math.e)
VM = pl.BlockSpec(memory_space=pltpu.VMEM)
ANY = pl.BlockSpec(memory_space=pl.ANY)


def dot(left, right, dims):
    return lax.dot_general(left, right, (dims, ((), ())), preferred_element_type=F32)


def mm(left, right):
    return dot(left, right, ((1,), (0,)))


def mm_t(left, right):
    return dot(left, right, ((1,), (1,)))


def t_mm(left, right):
    return dot(left, right, ((0,), (0,)))


def at(index, size):
    return pl.ds(pl.multiple_of(index * size, size), size)


def half_turn(values):
    return pltpu.roll(values, HEAD_DIM // 2, 1)


def head_norm(values):
    scaling = lax.rsqrt(jnp.mean(values * values, axis=-1, keepdims=True) + epsilon)
    return values * scaling, scaling


def head_prepare(values, gain, cosine, sine):
    normed = head_norm(values)[0] * gain
    return (normed * cosine + half_turn(normed) * sine).astype(BF)


def head_back(grad, values, gain, cosine, sine):
    normed, scaling = head_norm(values)
    turned = grad * cosine + half_turn(grad * sine)
    scaled = turned * gain
    inner = jnp.mean(scaled * normed, axis=-1, keepdims=True)
    return (
        scaling * (scaled - normed * inner),
        jnp.sum(turned * normed, axis=0, keepdims=True),
    )


def width_norm(residual):
    rate = lax.rsqrt(jnp.mean(residual * residual, axis=1, keepdims=True) + epsilon)
    return residual * rate, rate


class Net:
    def __init__(self, send, recv, limit):
        self.send, self.recv, self.limit, self.used = send, recv, limit, 0

    def copy(self, source, target, device):
        index = self.used
        self.used += 1
        assert index < self.limit
        made = pltpu.make_async_remote_copy(
            src_ref=source,
            dst_ref=target,
            send_sem=self.send.at[index],
            recv_sem=self.recv.at[index],
            device_id=device,
            device_id_type=MESH,
        )
        made.start()
        return made


def layers_kernel(sizes, shapes):
    dp, rows, cols = sizes
    group = rows * cols
    layers, tokens, block, head_cols, kv_cols, ff = shapes
    width = block * group
    slab = width // rows
    size = tokens // group
    q_heads, kv_heads = head_cols // HEAD_DIM, kv_cols // HEAD_DIM
    members = q_heads // kv_heads
    qkv_cols = head_cols + 2 * kv_cols
    q_block = min(SEQ_LEN, 256)
    limit = 256
    chip = rows * size

    pieces = []
    for layer in reversed(range(layers)):
        for name, extent, parts in (
            ("down", rows * ff, 2), ("gu", slab, 4), ("o", rows * head_cols, 2), ("qkv", slab, 4),
        ):
            for part in range(parts):
                pieces.append((name, layer, part * extent // parts, extent // parts))
    n_pieces = len(pieces)

    grad_shapes = {
        "down": (layers, rows * ff, slab),
        "gu": (layers, slab, 2 * rows * ff),
        "o": (layers, rows * head_cols, slab),
        "qkv": (layers, slab, rows * qkv_cols),
    }
    grad_names = list(grad_shapes)

    scratch = {
        "x0": ((group, tokens + 16, block), BF),
        "t0": ((group, tokens, block), BF),
        "fin": ((size, width), F32),
        "gains": ((8, width), F32),
        "mask": ((tokens, SEQ_LEN), F32),
        "wqkv": ((layers, width, qkv_cols), BF),
        "wo": ((layers, head_cols, width), BF),
        "wgu": ((layers, width, 2 * ff), BF),
        "wd": ((layers, ff, width), BF),
        "feat_a": ((layers, tokens, width), BF),
        "feat_f": ((layers, tokens, width), BF),
        "res": ((2 * layers, size, width), F32),
        "raw": ((layers, tokens, head_cols + kv_cols), F32),
        "prep": ((layers, tokens, qkv_cols), BF),
        "inv": ((tokens, HEAD_DIM), F32),
        "att": ((layers, rows, tokens, head_cols), BF),
        "gu": ((max(layers - 1, 1), tokens, 2 * ff), F32),
        "cos": ((tokens, HEAD_DIM), F32),
        "sin": ((tokens, HEAD_DIM), F32),
        "hid": ((layers, rows, tokens, ff), BF),
        "part": ((tokens, width), BF),
        "got_row": ((2, max(rows - 1, 1), cols, size, width), BF),
        "mid": ((max(cols - 1, 1), size, width), BF),
        "got_col": ((2, max(cols - 1, 1), size, width), BF),
        "gb": ((2, tokens, width), BF),
        "dgu": ((rows, tokens, 2 * ff), BF),
        "dqkv": ((rows, tokens, qkv_cols), BF),
        "datt": ((tokens, head_cols), BF),
        "dkv": ((2, tokens, HEAD_DIM), F32),
        "dq": ((tokens, HEAD_DIM), F32),
        "gtok": ((size, width), F32),
        "sums": ((group, 16, HEAD_DIM), F32),
        "sums_in": ((group, 16, HEAD_DIM), F32),
        "dsum": ((dp, 16, HEAD_DIM), F32),
    }
    for name in grad_names:
        scratch["acc_" + name] = (grad_shapes[name], BF)
        scratch["frm_" + name] = (grad_shapes[name], BF)
        scratch["tot_" + name] = (grad_shapes[name], BF)
    names = list(scratch)

    def kernel(
        x_ref, og_ref, again_ref, fgain_ref, qgain_ref, kgain_ref, pos_ref,
        wq_ref, wk_ref, wv_ref, wo_ref, wg_ref, wu_ref, wd_ref,
        out_ref, din_ref, small_ref, t_down, t_gu, t_o, t_qkv, *rest,
    ):
        ref = dict(zip(names, rest))
        send, recv, local, up_send, up_recv, in_send, in_recv, stored = rest[len(names):]
        totals = {name: ref["tot_" + name] for name in grad_names}
        results = dict(zip(grad_names, (t_down, t_gu, t_o, t_qkv)))
        cos_ref, sin_ref = ref["cos"], ref["sin"]
        net = Net(send, recv, limit)
        row, col, place = lax.axis_index("row"), lax.axis_index("col"), lax.axis_index("dp")
        me = row * cols + col
        row_peers = [lax.rem(row + step, rows) for step in range(1, rows)]
        col_peers = [lax.rem(col + step, cols) for step in range(1, cols)]
        others = [
            (lax.rem(row + down, rows), lax.rem(col + over, cols))
            for down in range(rows)
            for over in range(cols)
            if down or over
        ]

        staged = []
        counter = [0]

        def weight_moves(layer):
            return [
                (wq_ref, "wqkv", 1, head_cols, 0),
                (wk_ref, "wqkv", 1, kv_cols, head_cols),
                (wv_ref, "wqkv", 1, kv_cols, head_cols + kv_cols),
                (wo_ref, "wo", 0, head_cols, 0),
                (wg_ref, "wgu", 1, ff, 0),
                (wu_ref, "wgu", 1, ff, ff),
                (wd_ref, "wd", 0, ff, 0),
            ]

        def weight_pair(move, layer, owner):
            source, name, split, extent, start = move
            if split == 1:
                return (
                    source.at[layer, :, at(owner, extent)],
                    ref[name].at[layer, at(row, slab), pl.ds(start, extent)],
                )
            return (
                source.at[layer, at(owner, extent), :],
                ref[name].at[layer, :, at(row, slab)],
            )

        own_weights = {}
        for layer in range(layers):
            for move in weight_moves(layer):
                source, target = weight_pair(move, layer, row)
                copy = pltpu.make_async_copy(source, target, local.at[counter[0]])
                copy.start()
                counter[0] += 1
                own_weights.setdefault((layer, move[1]), []).append(copy)

        x0 = ref["x0"]
        gain = jnp.concatenate([again_ref[...], fgain_ref[...]], axis=0)
        high = gain.astype(BF)
        middle = (gain - high.astype(F32)).astype(BF)
        low = (gain - high.astype(F32) - middle.astype(F32)).astype(BF)
        zeros = jnp.zeros((16 - 3 * 2 * layers, block), BF)
        count = 2 * layers
        x0[me, pl.ds(0, tokens), :] = x_ref[...].astype(BF)
        x0[me, pl.ds(tokens, 16), :] = jnp.concatenate(
            [high[:count].astype(F32), middle[:count].astype(F32), low[:count].astype(F32),
             zeros.astype(F32)], axis=0
        ).astype(BF)

        barrier = pltpu.get_barrier_semaphore()
        greeted = [{"row": there[0], "col": there[1]} for there in others]
        greeted += [{"dp": lax.rem(place + step, dp)} for step in range(1, dp)]
        for peer in greeted:
            pl.semaphore_signal(barrier, inc=1, device_id=peer, device_id_type=MESH)
        pl.semaphore_wait(barrier, len(greeted))

        def gather_start(view):
            mine = view(row, col)
            over = [None] * cols
            for step in range(cols - 1, 0, -1):
                over[step] = net.copy(mine, mine, {"col": col_peers[step - 1]})
            down = [[net.copy(mine, mine, {"row": peer}) for peer in row_peers]]
            return view, over, down

        def gather_step(state, step):
            view, over, down = state
            if step:
                over[step].wait_recv()
                here = view(row, lax.rem(col + cols - step, cols))
                down.append([net.copy(here, here, {"row": peer}) for peer in row_peers])

        def gather_rows(state, step):
            for copy in state[2][step]:
                copy.wait_recv()

        def gather_end(state):
            for copy in state[1][1:]:
                copy.wait_send()
            for line in state[2]:
                for copy in line:
                    copy.wait_send()

        def gather_rest(state):
            for step in range(1, cols):
                gather_step(state, step)
            for step in range(cols):
                gather_rows(state, step)
            gather_end(state)

        def chip_rows(source, target):
            parts = [source[at(there * cols + target, size), :] for there in range(rows)]
            return jnp.concatenate(parts, axis=0) if rows > 1 else parts[0]

        def store_rows(target_ref, target, value):
            for there in range(rows):
                target_ref[at(there * cols + target, size), :] = value[
                    there * size : (there + 1) * size
                ]

        part, mid = ref["part"], ref["mid"]

        def scatter(compute, order, fill_a=None, gather=None, slots=0, idle=None):
            first, second = {}, {}
            got_row, got_col = ref["got_row"].at[slots], ref["got_col"].at[slots]

            def pair_sum(step):
                target = lax.rem(col + cols - step, cols)
                total = part[at(row * cols + target, size), :].astype(F32)
                for slot in range(rows - 1):
                    first[slot, step].wait_recv()
                    total += got_row[slot, step].astype(F32)
                return total

            def forward(step):
                mid[step - 1] = pair_sum(step).astype(BF)
                target = lax.rem(col + cols - step, cols)
                second[step] = net.copy(mid.at[step - 1], got_col.at[step - 1], {"col": target})

            waiting = []
            for step in order:
                target = lax.rem(col + cols - step, cols)
                if gather is not None:
                    gather_step(gather, step)
                    if step == cols - 1 and idle is not None:
                        idle()
                    gather_rows(gather, step)
                store_rows(part, target, compute(target).astype(BF))
                for slot, peer in enumerate(row_peers):
                    first[slot, step] = net.copy(
                        part.at[at(peer * cols + target, size), :],
                        got_row.at[slot, step],
                        {"row": peer},
                    )
                if waiting:
                    forward(waiting.pop())
                if step:
                    waiting.append(step)
            for step in waiting:
                forward(step)
            if gather is not None:
                gather_end(gather)
            if fill_a is not None:
                fill_a()
            total = pair_sum(0)
            for step in range(1, cols):
                second[step].wait_recv()
                total += got_col[step - 1].astype(F32)
            for copy in list(first.values()) + list(second.values()):
                copy.wait_send()
            return total

        late = list(range(1, cols)) + [0]
        early = list(range(cols))

        def feature_view(buffer):
            return lambda at_row, at_col: buffer.at[at_row * cols + at_col]

        def token_view(buffer):
            return lambda at_row, at_col: buffer.at[at(at_row * cols + at_col, size), :]

        first_gather = gather_start(feature_view(x0))

        sent_weights = {}

        def send_weights(layer):
            for move in weight_moves(layer):
                for peer in row_peers:
                    source, target = weight_pair(move, layer, peer)
                    sent_weights.setdefault((layer, move[1]), []).append(
                        net.copy(source, target, {"row": peer})
                    )

        def need_weight(layer, name):
            for copy in own_weights.pop((layer, name), []):
                copy.wait()
            for copy in sent_weights.pop((layer, name), []):
                copy.wait()

        def to_tokens(source, target):
            copies = []
            for there in others:
                index = there[0] * cols + there[1]
                copies.append(
                    net.copy(
                        source.at[at(index, size), :],
                        target.at[:, at(me, block)],
                        {"row": there[0], "col": there[1]},
                    )
                )
            target[:, at(me, block)] = source[at(me, size), :]
            return copies

        def to_features(source, target):
            copies = []
            for there in others:
                index = there[0] * cols + there[1]
                copies.append(
                    net.copy(
                        source.at[:, at(index, block)],
                        target.at[at(me, size), :],
                        {"row": there[0], "col": there[1]},
                    )
                )
            target[at(me, size), :] = source[:, at(me, block)]
            return copies

        send_weights(0)

        lane = lax.broadcasted_iota(jnp.int32, (128, HEAD_DIM), 1)
        low_half = lane < HEAD_DIM // 2
        exponent = jnp.where(low_half, lane, lane - HEAD_DIM // 2).astype(F32)
        inverse = jnp.exp2(exponent * (-2.0 * math.log2(rope_base) / HEAD_DIM))
        for index in range(tokens // 128):
            here = slice(index * 128, (index + 1) * 128)
            spot = jnp.broadcast_to(pos_ref[index : index + 1, :].astype(F32), (128, 128)).T
            angle = spot * inverse
            ref["cos"][here, :] = jnp.cos(angle)
            turn = jnp.sin(angle)
            ref["sin"][here, :] = jnp.where(low_half, -turn, turn)
            begin = index * 128 % SEQ_LEN
            for start in range(0, SEQ_LEN, 128):
                offset = (
                    begin - start
                    + lax.broadcasted_iota(jnp.int32, (128, 128), 0)
                    - lax.broadcasted_iota(jnp.int32, (128, 128), 1)
                ).astype(F32)
                seen = (offset >= 0.0) & (offset <= spot)
                ref["mask"][here, start : start + 128] = jnp.where(seen, 0.0, masked_score)

        gather_rest(first_gather)
        residual_moves = to_tokens(x_ref, ref["res"].at[0])

        gains = ref["gains"]
        for slot in range(group):
            split = x0[slot, pl.ds(tokens, 16), :].astype(F32)
            gains[0:count, slot * block : (slot + 1) * block] = (
                split[:count] + split[count : 2 * count] + split[2 * count : 3 * count]
            )

        for start in range(0, tokens, 128):
            length = pl.ds(start, 128)
            squares = jnp.zeros((128, block), F32)
            for slot in range(group):
                value = x0[slot, length, :].astype(F32)
                squares += value * value
            rate = lax.rsqrt(jnp.sum(squares, axis=1, keepdims=True) * (1.0 / width) + epsilon)
            for slot in range(group):
                lanes = slice(slot * block, (slot + 1) * block)
                ref["feat_a"][0, length, lanes] = (
                    x0[slot, length, :].astype(F32) * rate * gains[0:1, lanes]
                ).astype(BF)

        state = {}

        def attend(layer):
            raw, prep, att = (ref[k].at[layer] for k in ("raw", "prep", "att"))
            inv = ref["inv"]
            gain_q, gain_k = qgain_ref[layer : layer + 1], kgain_ref[layer : layer + 1]
            cosine, sine = cos_ref[...], sin_ref[...]
            for head in range(q_heads + kv_heads):
                lanes = slice(head * HEAD_DIM, (head + 1) * HEAD_DIM)
                gain_h = gain_q if head < q_heads else gain_k
                prep[:, lanes] = head_prepare(raw[:, lanes], gain_h, cosine, sine)
            for start in range(0, tokens, SEQ_LEN):
                for head in range(q_heads):
                    kv = head // members
                    k_lanes = slice(head_cols + kv * HEAD_DIM, head_cols + (kv + 1) * HEAD_DIM)
                    v_at = head_cols + kv_cols + kv * HEAD_DIM
                    v_lanes = slice(v_at, v_at + HEAD_DIM)
                    lanes = slice(head * HEAD_DIM, (head + 1) * HEAD_DIM)
                    for begin in range(0, SEQ_LEN, q_block):
                        mine = pl.ds(start + begin, q_block)
                        keys = pl.ds(start, begin + q_block)
                        scores = mm_t(prep[mine, lanes], prep[keys, k_lanes])
                        weights = jnp.exp2(
                            scores * (SCALE * LOG2E)
                            + ref["mask"][mine, 0 : begin + q_block]
                        )
                        inverse = 1.0 / jnp.sum(weights, axis=-1, keepdims=True)
                        lane = layer * q_heads + head
                        inv[mine, lane : lane + 1] = inverse
                        att[row, mine, lanes] = mm(
                            (weights * inverse).astype(BF), prep[keys, v_lanes]
                        ).astype(BF)

        def feature_block(value, gain_row, target):
            normed, rate = width_norm(value)
            target[at(me, size), :] = (normed * gains[gain_row : gain_row + 1, :]).astype(BF)

        def send_row(buffer):
            return [net.copy(buffer.at[row], buffer.at[row], {"row": peer}) for peer in row_peers]

        top_gathers = []
        top_parts = 4

        def top_start():
            extent = tokens // top_parts
            here = pl.ds(len(top_gathers) * extent, extent)
            top_gathers.append(
                gather_start(
                    lambda at_row, at_col: ref["t0"].at[at_row * cols + at_col, here, :]
                )
            )

        def top_forward(index):
            for step in range(1, cols):
                gather_step(top_gathers[index], step)

        ref["t0"][me] = og_ref[...].astype(BF)
        top_start()
        top_start()
        row_moves = {}
        last = layers - 1

        def feed_forward(layer, target):
            feat = chip_rows(ref["feat_f"].at[layer], target)
            both = mm(feat, ref["wgu"][layer])
            gate, up = both[:, :ff], both[:, ff:]
            sig = lax.logistic(gate)
            hidden = (gate * sig * up).astype(BF)
            store_rows(ref["hid"].at[layer, row], target, hidden)
            return both, gate, up, sig, hidden

        for layer in range(layers):
            feat_a, feat_f = ref["feat_a"].at[layer], ref["feat_f"].at[layer]
            raw = ref["raw"].at[layer]
            need_weight(layer, "wqkv")
            for start in range(0, tokens, 256):
                here = slice(start, start + 256)
                value = mm(feat_a[here, :], ref["wqkv"][layer])
                raw[here, :] = value[:, : head_cols + kv_cols]
                ref["prep"][layer, here, head_cols + kv_cols :] = value[
                    :, head_cols + kv_cols :
                ].astype(BF)
            if layer == 0:
                for extra in range(1, layers):
                    send_weights(extra)
            attend(layer)
            need_weight(layer, "wo")

            def compute_o(target, layer=layer):
                return mm(chip_rows(ref["att"].at[layer, row], target), ref["wo"][layer])

            def during_o(layer=layer):
                row_moves["att", layer] = send_row(ref["att"].at[layer])
                if layer == last:
                    top_forward(3)

            total = scatter(compute_o, late, fill_a=during_o)
            if layer == 0:
                for copy in residual_moves:
                    copy.wait()
            ref["res"][2 * layer + 1] = ref["res"][2 * layer] + total
            feature_block(ref["res"][2 * layer + 1], layers + layer, feat_f)
            gathering = gather_start(token_view(feat_f))
            need_weight(layer, "wgu")
            need_weight(layer, "wd")
            if layer == last:
                break

            def compute_ff(target, layer=layer):
                both, gate, up, sig, hidden = feed_forward(layer, target)
                store_rows(ref["gu"].at[layer], target, both)
                return mm(hidden, ref["wd"][layer])

            def during_ff(layer=layer):
                row_moves["hid", layer] = send_row(ref["hid"].at[layer])

            def idle_ff(layer=layer):
                if layer == 0:
                    top_start()
                    top_forward(0)
                    top_forward(1)

            total = scatter(compute_ff, early, fill_a=during_ff, gather=gathering, idle=idle_ff)
            ref["res"][2 * layer + 2] = ref["res"][2 * layer + 1] + total
            feature_block(ref["res"][2 * layer + 2], layer + 1, ref["feat_a"].at[layer + 1])
            coming = gather_start(token_view(ref["feat_a"].at[layer + 1]))
            for step in range(1, cols):
                gather_step(coming, step)
            if layer == 0:
                top_start()
                top_forward(2)
                grad_moves = to_tokens(og_ref, ref["gtok"])
            for step in range(cols):
                gather_rows(coming, step)
            gather_end(coming)

        half = dp // 2
        on_left = place < half
        depth = jnp.where(on_left, place, dp - 1 - place)
        inward = jnp.where(on_left, place + 1, place - 1)
        outward = jnp.where(on_left, place - 1, place + 1)
        outward = jnp.clip(outward, 0, dp - 1)
        is_mid = depth == half - 1
        inner = depth > 0

        def views(index):
            name, layer, start, extent = pieces[index]
            rows_at = pl.ds(start, extent)
            return (
                ref["acc_" + name].at[layer, rows_at, :],
                ref["frm_" + name].at[layer, rows_at, :],
                totals[name].at[layer, rows_at, :],
            )

        def hop(source, target, index, kind, peer):
            sems = {
                "up": (up_send, up_recv),
                "across": (up_send, in_recv),
                "back": (in_send, in_recv),
            }[kind]
            return pltpu.make_async_remote_copy(
                src_ref=source,
                dst_ref=target,
                send_sem=sems[0].at[index],
                recv_sem=sems[1].at[index],
                device_id={"dp": peer},
                device_id_type=MESH,
            )

        def send_inward(index, condition):
            acc, frm, tot = views(index)

            @pl.when(condition & jnp.logical_not(is_mid))
            def _():
                hop(acc, frm, index, "up", inward).start()

            @pl.when(condition & is_mid)
            def _():
                hop(acc, tot, index, "across", inward).start()

        def add_into(target, one, two):
            extent = one.shape[0]
            chunk = 32

            def body(step, carry):
                here = at(step, chunk)
                target[here, :] = (one[here, :].astype(F32) + two[here, :].astype(F32)).astype(BF)
                return carry

            lax.fori_loop(0, extent // chunk, body, 0)

        window, lag = 2, 2

        def up(index):
            if index >= window:
                acc, frm, tot = views(index - window)

                @pl.when(jnp.logical_not(inner))
                def _():
                    hop(acc, frm, index - window, "up", inward).wait_send()

            send_inward(index, jnp.logical_not(inner))

        def across(index):
            acc, frm, tot = views(index)

            @pl.when(inner)
            def _():
                hop(acc, frm, index, "up", inward).wait_recv()
                add_into(acc, acc, frm)

            send_inward(index, inner)

        def back(index):
            acc, frm, tot = views(index)

            @pl.when(is_mid)
            def _():
                hop(acc, tot, index, "across", inward).wait_recv()
                add_into(tot, acc, tot)

            @pl.when(is_mid & inner)
            def _():
                hop(tot, tot, index, "back", outward).start()

        def outer(index):
            acc, frm, tot = views(index)

            @pl.when(jnp.logical_not(is_mid))
            def _():
                hop(tot, tot, index, "back", inward).wait_recv()

            @pl.when(jnp.logical_not(is_mid) & inner)
            def _():
                hop(tot, tot, index, "back", outward).start()

        done = {"made": 0, "steps": 0}

        def made(count_new):
            done["made"] += count_new

        def line_step(delay):
            step = done["steps"]
            done["steps"] += 1
            for action, behind in zip((up, across, back), (0, delay, delay + 1)):
                if step - behind >= 0 and step - behind < n_pieces and (step - behind, action) not in done:
                    done[step - behind, action] = True
                    action(step - behind)

        def pump(count_steps=1):
            for _ in range(count_steps):
                if done["steps"] < done["made"]:
                    line_step(lag)

        def finish():
            while done["steps"] < n_pieces + lag + 1:
                line_step(lag)
            stores = []
            for index in range(n_pieces):
                outer(index)
                name, layer, start, extent = pieces[index]
                here = pl.ds(start, extent)
                copy = pltpu.make_async_copy(
                    totals[name].at[layer, here, :], results[name].at[layer, here, :],
                    stored.at[index],
                )
                copy.start()
                stores.append(copy)
            for copy in stores:
                copy.wait()
            for index in range(n_pieces):
                acc, frm, tot = views(index)
                if index < n_pieces - window:
                    @pl.when(inner)
                    def _(index=index, acc=acc, frm=frm):
                        hop(acc, frm, index, "up", inward).wait_send()
                else:
                    hop(acc, frm, index, "up", inward).wait_send()

                @pl.when(inner)
                def _(index=index, tot=tot):
                    hop(tot, tot, index, "back", outward).wait_send()

        gb, gb2 = ref["gb"].at[0], ref["gb"].at[1]
        for index in range(top_parts):
            for step in range(cols):
                gather_rows(top_gathers[index], step)
            gather_end(top_gathers[index])
        for slot in range(group):
            gb[:, slot * block : (slot + 1) * block] = ref["t0"][slot]
        gtok, sums = ref["gtok"], ref["sums"]
        for slot in range(group):
            sums[slot] = jnp.zeros((16, HEAD_DIM), F32)

        def slab_of(source):
            return source[:, at(row, slab)]

        quarter = slab // 4

        def slab_part(source, index):
            start = pl.multiple_of(row * slab + index * quarter, quarter)
            return source[:, pl.ds(start, quarter)]

        def norm_back(total, residual, gain_row):
            normed, rate = width_norm(residual)
            scaled = total * gains[gain_row : gain_row + 1, :]
            inner_mean = jnp.mean(scaled * normed, axis=1, keepdims=True)
            gtok[...] = gtok[...] + rate * (scaled - normed * inner_mean)
            line = jnp.sum(total * normed, axis=0, keepdims=True)
            for slot in range(group):
                sums[slot, gain_row : gain_row + 1, :] = line[:, slot * block : (slot + 1) * block]

        def attend_back(layer):
            raw, prep, att = (ref[k].at[layer] for k in ("raw", "prep", "att"))
            inv = ref["inv"]
            gain_q, gain_k = qgain_ref[layer : layer + 1], kgain_ref[layer : layer + 1]
            dqkv, datt = ref["dqkv"], ref["datt"]
            dk, dv, dq = ref["dkv"].at[0], ref["dkv"].at[1], ref["dq"]
            cosine, sine = cos_ref[...], sin_ref[...]
            total_q = jnp.zeros((1, HEAD_DIM), F32)
            total_k = jnp.zeros((1, HEAD_DIM), F32)
            for kv in range(kv_heads):
                k_lanes = slice(head_cols + kv * HEAD_DIM, head_cols + (kv + 1) * HEAD_DIM)
                v_at = head_cols + kv_cols + kv * HEAD_DIM
                v_lanes = slice(v_at, v_at + HEAD_DIM)
                dk[...] = jnp.zeros((tokens, HEAD_DIM), F32)
                dv[...] = jnp.zeros((tokens, HEAD_DIM), F32)
                for member in range(members):
                    head = kv * members + member
                    lanes = slice(head * HEAD_DIM, (head + 1) * HEAD_DIM)
                    lane = layer * q_heads + head
                    for start in range(0, tokens, SEQ_LEN):
                        for begin in range(0, SEQ_LEN, q_block):
                            mine = pl.ds(start + begin, q_block)
                            keys = pl.ds(start, begin + q_block)
                            scores = mm_t(prep[mine, lanes], prep[keys, k_lanes])
                            probs = jnp.exp2(
                                scores * (SCALE * LOG2E)
                                + ref["mask"][mine, 0 : begin + q_block]
                            ) * inv[mine, lane : lane + 1]
                            grad_o = datt[mine, lanes]
                            inner_sum = jnp.sum(
                                grad_o.astype(F32) * att[row, mine, lanes].astype(F32),
                                axis=-1,
                                keepdims=True,
                            )
                            dv[keys, :] += t_mm(probs.astype(BF), grad_o)
                            grad_s = (
                                probs * (mm_t(grad_o, prep[keys, v_lanes]) - inner_sum)
                            ).astype(BF)
                            dq[mine, :] = mm(grad_s, prep[keys, k_lanes]) * SCALE
                            dk[keys, :] += t_mm(grad_s, prep[mine, lanes])
                    back, line = head_back(dq[...], raw[:, lanes], gain_q, cosine, sine)
                    dqkv[row, :, lanes] = back.astype(BF)
                    total_q += line
                back, line = head_back(dk[...] * SCALE, raw[:, k_lanes], gain_k, cosine, sine)
                dqkv[row, :, k_lanes] = back.astype(BF)
                dqkv[row, :, v_lanes] = dv[...].astype(BF)
                total_k += line
            at_row = 8 + 2 * layer
            for slot in range(group):
                sums[slot, at_row : at_row + 1, :] = total_q
                sums[slot, at_row + 1 : at_row + 2, :] = total_k

        for layer in reversed(range(layers)):
            feat_a, feat_f = ref["feat_a"].at[layer], ref["feat_f"].at[layer]
            if layer != last:
                gb[at(me, size), :] = gtok[...].astype(BF)
                gathering = gather_start(token_view(gb))

            def compute_ff_back(target, layer=layer):
                grad = chip_rows(gb, target)
                if layer == last:
                    both, gate, up, sig, hidden = feed_forward(layer, target)
                else:
                    both = chip_rows(ref["gu"].at[layer], target)
                    gate, up = both[:, :ff], both[:, ff:]
                    sig = lax.logistic(gate)
                dhid = mm_t(grad, ref["wd"][layer])
                dgate = (dhid * up * sig * (1.0 + gate * (1.0 - sig))).astype(BF)
                dup = (dhid * gate * sig).astype(BF)
                joined = jnp.concatenate([dgate, dup], axis=1)
                store_rows(ref["dgu"].at[row], target, joined)
                return mm_t(joined, ref["wgu"][layer])

            def ffn_grads(layer=layer, feat_f=feat_f):
                if layer == last:
                    row_moves["hid", layer] = send_row(ref["hid"].at[layer])
                moves = send_row(ref["dgu"])
                for copy in row_moves.pop(("hid", layer)):
                    copy.wait()
                right = slab_of(gb)
                for there in range(rows):
                    ref["acc_down"][layer, there * ff : (there + 1) * ff, :] = t_mm(
                        ref["hid"][layer, there], right
                    ).astype(BF)
                made(2)
                pump(2)
                for copy in moves:
                    copy.wait()
                for index in range(4):
                    left = slab_part(feat_f, index)
                    here = slice(index * quarter, (index + 1) * quarter)
                    for there in range(rows):
                        value = t_mm(left, ref["dgu"][there]).astype(BF)
                        ref["acc_gu"][layer, here, there * ff : (there + 1) * ff] = value[:, :ff]
                        begin = (rows + there) * ff
                        ref["acc_gu"][layer, here, begin : begin + ff] = value[:, ff:]
                made(4)
                pump()

            total = scatter(compute_ff_back, early, fill_a=ffn_grads, gather=gathering)
            if layer == last:
                for copy in grad_moves:
                    copy.wait()
            norm_back(total, ref["res"][2 * layer + 1], layers + layer)
            gb2[at(me, size), :] = gtok[...].astype(BF)
            gathering = gather_start(token_view(gb2))
            pump()
            gather_rest(gathering)
            pump()
            for start in range(0, tokens, 256):
                ref["datt"][start : start + 256, :] = mm_t(
                    gb2[start : start + 256, :], ref["wo"][layer]
                ).astype(BF)
            attend_back(layer)
            pump()
            moves = send_row(ref["dqkv"])

            def compute_qkv_back(target, layer=layer):
                return mm_t(chip_rows(ref["dqkv"].at[row], target), ref["wqkv"][layer])

            def attn_grads(layer=layer, feat_a=feat_a, moves=moves):
                for copy in row_moves.pop(("att", layer)):
                    copy.wait()
                right = slab_of(gb2)
                for there in range(rows):
                    ref["acc_o"][layer, there * head_cols : (there + 1) * head_cols, :] = t_mm(
                        ref["att"][layer, there], right
                    ).astype(BF)
                made(2)
                pump()
                for copy in moves:
                    copy.wait()
                acc = ref["acc_qkv"]
                for index in range(4):
                    left = slab_part(feat_a, index)
                    here = slice(index * quarter, (index + 1) * quarter)
                    for there in range(rows):
                        value = t_mm(left, ref["dqkv"][there]).astype(BF)
                        begin = there * head_cols
                        acc[layer, here, begin : begin + head_cols] = value[:, :head_cols]
                        begin = rows * head_cols + there * kv_cols
                        acc[layer, here, begin : begin + kv_cols] = value[
                            :, head_cols : head_cols + kv_cols
                        ]
                        begin += rows * kv_cols
                        acc[layer, here, begin : begin + kv_cols] = value[:, head_cols + kv_cols :]
                made(4)
                pump()

            total = scatter(compute_qkv_back, late, fill_a=attn_grads)
            norm_back(total, ref["res"][2 * layer], layer)
            pump()

        sums_in, dsum = ref["sums_in"], ref["dsum"]
        sum_moves = []
        for there in others:
            index = there[0] * cols + there[1]
            sum_moves.append(
                net.copy(sums.at[index], sums_in.at[me], {"row": there[0], "col": there[1]})
            )
        sums_in[me] = sums[me]
        din_moves = to_features(gtok, din_ref)

        def compute_down(target):
            return mm(chip_rows(ref["hid"].at[last, row], target), ref["wd"][last])

        pump()
        result = scatter(compute_down, late, slots=1)
        ref["fin"][...] = ref["res"][2 * last + 1] + result
        out_moves = to_features(ref["fin"], out_ref)
        for copy in sum_moves:
            copy.wait()
        total = sums_in[0]
        for slot in range(1, group):
            total += sums_in[slot]
        dsum[place] = total
        sum_moves = [
            net.copy(dsum.at[place], dsum.at[place], {"dp": lax.rem(place + step, dp)})
            for step in range(1, dp)
        ]
        for copy in din_moves + out_moves:
            copy.wait()
        for copy in sum_moves:
            copy.wait()
        total = dsum[0]
        for slot in range(1, dp):
            total += dsum[slot]
        small_ref[...] = total
        finish()

    def call(*operands):
        shapes_out = [
            jax.ShapeDtypeStruct((tokens, block), F32),
            jax.ShapeDtypeStruct((tokens, block), F32),
            jax.ShapeDtypeStruct((16, HEAD_DIM), F32),
        ] + [jax.ShapeDtypeStruct(grad_shapes[name], BF) for name in grad_names]
        return pl.pallas_call(
            kernel,
            name="layers",
            out_shape=shapes_out,
            in_specs=[VM] * 7 + [ANY] * 7,
            out_specs=[VM] * 3 + [ANY] * len(grad_names),
            scratch_shapes=[pltpu.VMEM(*scratch[name]) for name in names]
            + [
                pltpu.SemaphoreType.DMA((limit,)),
                pltpu.SemaphoreType.DMA((limit,)),
                pltpu.SemaphoreType.DMA((7 * layers,)),
            ]
            + [pltpu.SemaphoreType.DMA((n_pieces,))] * 5,
            compiler_params=pltpu.CompilerParams(
                collective_id=1, has_side_effects=True, vmem_limit_bytes=60 << 20
            ),
        )(*operands)

    return call


def per_device(
    sizes,
    residual_in,
    positions,
    attn_gain,
    query_weight,
    key_weight,
    value_weight,
    query_gain,
    key_gain,
    output_weight,
    ffn_gain,
    gate_weight,
    up_weight,
    down_weight,
    output_grad,
):
    dp, rows, cols = sizes
    layers = query_weight.shape[0]
    tokens, block = residual_in.shape
    shapes = (
        layers, tokens, block, query_weight.shape[2] // rows, key_weight.shape[2] // rows,
        gate_weight.shape[2] // rows,
    )
    outputs, input_grad, small, down, gu, out_w, qkv = layers_kernel(sizes, shapes)(
        residual_in, output_grad, attn_gain, ffn_gain, query_gain, key_gain,
        positions.reshape(tokens // 128, 128),
        query_weight, key_weight, value_weight, output_weight, gate_weight, up_weight, down_weight,
    )
    return widen(
        outputs, input_grad, small, down, gu, out_w, qkv,
        (query_weight.shape[2], key_weight.shape[2], gate_weight.shape[2]),
    )


def widen(outputs, input_grad, small, down, gu, out_w, qkv, columns):
    wide_q, wide_k, wide_f = columns
    layers, parts = down.shape[0], 4
    tokens, block = outputs.shape

    def kernel(
        out_in, din_in, small_in, down_in, gu_in, o_in, qkv_in,
        out_ref, din_ref, again_ref, q_ref, k_ref, v_ref, qgain_ref, kgain_ref, o_ref, fgain_ref,
        gate_ref, up_ref, down_ref,
    ):
        out_ref[...] = out_in[...]
        din_ref[...] = din_in[...]
        again_ref[...] = small_in[0:layers, :]
        fgain_ref[...] = small_in[layers : 2 * layers, :]
        for layer in range(layers):
            start = 8 + 2 * layer
            qgain_ref[layer : layer + 1, :] = small_in[start : start + 1, :]
            kgain_ref[layer : layer + 1, :] = small_in[start + 1 : start + 2, :]
        q_ref[...] = qkv_in[:, :, :wide_q].astype(F32)
        k_ref[...] = qkv_in[:, :, wide_q : wide_q + wide_k].astype(F32)
        v_ref[...] = qkv_in[:, :, wide_q + wide_k :].astype(F32)
        o_ref[...] = o_in[...].astype(F32)
        gate_ref[...] = gu_in[:, :, :wide_f].astype(F32)
        up_ref[...] = gu_in[:, :, wide_f:].astype(F32)
        down_ref[...] = down_in[...].astype(F32)

    flat = pl.BlockSpec((tokens // (layers * parts), block), lambda i, j: (i * parts + j, 0))

    def whole(shape):
        return pl.BlockSpec(shape, lambda i, j: (0,) * len(shape))

    def cut(height, width):
        return pl.BlockSpec((1, height // parts, width), lambda i, j: (i, j, 0))

    def shape_of(*extent):
        return jax.ShapeDtypeStruct(extent, F32)

    slab, wide_d = qkv.shape[1], down.shape[1]
    wide_o, out_cols = out_w.shape[1:]
    gain = (layers, block)
    head_gain = (layers, HEAD_DIM)
    return pl.pallas_call(
        kernel,
        name="widen",
        grid=(layers, parts),
        in_specs=[
            flat, flat, whole(small.shape), cut(wide_d, out_cols), cut(slab, gu.shape[2]),
            cut(wide_o, out_cols), cut(slab, qkv.shape[2]),
        ],
        out_specs=[
            flat, flat, whole(gain), cut(slab, wide_q), cut(slab, wide_k), cut(slab, wide_k),
            whole(head_gain), whole(head_gain), cut(wide_o, out_cols), whole(gain),
            cut(slab, wide_f), cut(slab, wide_f), cut(wide_d, out_cols),
        ],
        out_shape=[
            shape_of(tokens, block), shape_of(tokens, block), shape_of(*gain),
            shape_of(layers, slab, wide_q), shape_of(layers, slab, wide_k),
            shape_of(layers, slab, wide_k), shape_of(*head_gain), shape_of(*head_gain),
            shape_of(layers, wide_o, out_cols), shape_of(*gain),
            shape_of(layers, slab, wide_f), shape_of(layers, slab, wide_f),
            shape_of(layers, wide_d, out_cols),
        ],
        compiler_params=pltpu.CompilerParams(vmem_limit_bytes=40 << 20),
    )(outputs, input_grad, small, down, gu, out_w, qkv)


def solution(mesh):
    wide = P("dp", ("row", "col"))
    gain = P(None, ("row", "col"))
    into, out_of = P(None, "row", "col"), P(None, "col", "row")
    in_specs = (
        wide, P("dp"), gain, into, into, into, P(), P(), out_of, gain, into, into, out_of, wide,
    )
    out_specs = (wide, wide, gain, into, into, into, P(), P(), out_of, gain, into, into, out_of)
    return jax.shard_map(
        functools.partial(per_device, (mesh.shape["dp"], mesh.shape["row"], mesh.shape["col"])),
        mesh=mesh,
        in_specs=in_specs,
        out_specs=out_specs,
        check_vma=False,
    )
```

```python
import functools
import math

import jax
import jax.numpy as jnp
from jax import lax
from jax.experimental import pallas as pl
from jax.experimental.pallas import tpu as pltpu
from jax.sharding import PartitionSpec as P

HEAD_DIM = 128
SEQ_LEN = 512

SUM_WINDOW = 3
epsilon = 1e-06
rope_base = 1000000.0
masked_score = -1e30
MESH = pl.DeviceIdType.MESH
BF = jnp.bfloat16
F32 = jnp.float32
SCALE = HEAD_DIM ** (-0.5)
LOG2E = math.log2(math.e)
VM = pl.BlockSpec(memory_space=pltpu.VMEM)
ANY = pl.BlockSpec(memory_space=pl.ANY)


def dot(left, right, dims):
    return lax.dot_general(left, right, (dims, ((), ())), preferred_element_type=F32)


def mm(left, right):
    return dot(left, right, ((1,), (0,)))


def mm_t(left, right):
    return dot(left, right, ((1,), (1,)))


def t_mm(left, right):
    return dot(left, right, ((0,), (0,)))


def at(index, size):
    return pl.ds(pl.multiple_of(index * size, size), size)


def half_turn(values):
    return pltpu.roll(values, HEAD_DIM // 2, 1)


def head_norm(values):
    scaling = lax.rsqrt(jnp.mean(values * values, axis=-1, keepdims=True) + epsilon)
    return values * scaling, scaling


def head_prepare(values, gain, cosine, sine):
    normed = head_norm(values)[0] * gain
    return (normed * cosine + half_turn(normed) * sine).astype(BF)


def head_back(grad, values, gain, cosine, sine):
    normed, scaling = head_norm(values)
    turned = grad * cosine + half_turn(grad * sine)
    scaled = turned * gain
    inner = jnp.mean(scaled * normed, axis=-1, keepdims=True)
    return (
        scaling * (scaled - normed * inner),
        jnp.sum(turned * normed, axis=0, keepdims=True),
    )


def width_norm(residual):
    rate = lax.rsqrt(jnp.mean(residual * residual, axis=1, keepdims=True) + epsilon)
    return residual * rate, rate


class Net:
    def __init__(self, send, recv, limit):
        self.send, self.recv, self.limit, self.used = send, recv, limit, {}

    def copy(self, source, target, device, key=None):
        index = self.used.setdefault(len(self.used) if key is None else key, len(self.used))
        assert index < self.limit
        made = pltpu.make_async_remote_copy(
            src_ref=source,
            dst_ref=target,
            send_sem=self.send.at[index],
            recv_sem=self.recv.at[index],
            device_id=device,
            device_id_type=MESH,
        )
        made.start()
        return made


def layers_kernel(sizes, shapes):
    dp, rows, cols = sizes
    group = rows * cols
    layers, tokens, block, head_cols, kv_cols, ff = shapes
    width = block * group
    slab = width // rows
    size = tokens // group
    q_heads, kv_heads = head_cols // HEAD_DIM, kv_cols // HEAD_DIM
    members = q_heads // kv_heads
    qkv_cols = head_cols + 2 * kv_cols
    q_block = min(SEQ_LEN, 256)
    limit = 107 + dp
    chip = rows * size

    pieces = []
    for layer in reversed(range(layers)):
        for name, extent, parts in (
            ("down", rows * ff, 2), ("gu", slab, 4), ("o", rows * head_cols, 2), ("qkv", slab, 4),
        ):
            for part in range(parts):
                pieces.append((name, layer, part * extent // parts, extent // parts))
    n_pieces = len(pieces)

    grad_shapes = {
        "down": (layers, rows * ff, slab),
        "gu": (layers, slab, 2 * rows * ff),
        "o": (layers, rows * head_cols, slab),
        "qkv": (layers, slab, rows * qkv_cols),
    }
    grad_names = list(grad_shapes)

    scratch = {
        "x0": ((group, tokens + 16, block), BF),
        "t0": ((group, tokens, block), BF),
        "fin": ((size, width), F32),
        "gains": ((8, width), F32),
        "mask": ((tokens, SEQ_LEN), F32),
        "wqkv": ((layers, width, qkv_cols), BF),
        "wo": ((layers, head_cols, width), BF),
        "wgu": ((layers, width, 2 * ff), BF),
        "wd": ((layers, ff, width), BF),
        "feat_a": ((layers, tokens, width), BF),
        "feat_f": ((layers, tokens, width), BF),
        "res": ((2 * layers, size, width), F32),
        "raw": ((layers, tokens, head_cols + kv_cols), F32),
        "prep": ((layers, tokens, qkv_cols), BF),
        "inv": ((tokens, HEAD_DIM), F32),
        "att": ((layers, rows, tokens, head_cols), BF),
        "gu": ((max(layers - 1, 1), tokens, 2 * ff), F32),
        "cos": ((tokens, HEAD_DIM), F32),
        "sin": ((tokens, HEAD_DIM), F32),
        "hid": ((layers, rows, tokens, ff), BF),
        "part": ((tokens, width), BF),
        "got_row": ((2, max(rows - 1, 1), cols, size, width), BF),
        "mid": ((max(cols - 1, 1), size, width), BF),
        "got_col": ((2, max(cols - 1, 1), size, width), BF),
        "gb": ((2, tokens, width), BF),
        "dgu": ((rows, tokens, 2 * ff), BF),
        "dqkv": ((rows, tokens, qkv_cols), BF),
        "datt": ((tokens, head_cols), BF),
        "dkv": ((2, tokens, HEAD_DIM), F32),
        "dq": ((tokens, HEAD_DIM), F32),
        "gtok": ((size, width), F32),
        "sums": ((group, 16, HEAD_DIM), F32),
        "sums_in": ((group, 16, HEAD_DIM), F32),
        "dsum": ((dp, 16, HEAD_DIM), F32),
    }
    for name in grad_names:
        scratch["acc_" + name] = (grad_shapes[name], BF)
        scratch["frm_" + name] = (grad_shapes[name], BF)
        scratch["tot_" + name] = (grad_shapes[name], BF)
    names = list(scratch)

    def kernel(
        x_ref, og_ref, again_ref, fgain_ref, qgain_ref, kgain_ref, pos_ref,
        wq_ref, wk_ref, wv_ref, wo_ref, wg_ref, wu_ref, wd_ref,
        out_ref, din_ref, small_ref, t_down, t_gu, t_o, t_qkv, *rest,
    ):
        ref = dict(zip(names, rest))
        send, recv, local, up_send, up_recv, in_send, in_recv, stored = rest[len(names):]
        totals = {name: ref["tot_" + name] for name in grad_names}
        results = dict(zip(grad_names, (t_down, t_gu, t_o, t_qkv)))
        cos_ref, sin_ref = ref["cos"], ref["sin"]
        net = Net(send, recv, limit)
        row, col, place = lax.axis_index("row"), lax.axis_index("col"), lax.axis_index("dp")
        me = row * cols + col
        row_peers = [lax.rem(row + step, rows) for step in range(1, rows)]
        col_peers = [lax.rem(col + step, cols) for step in range(1, cols)]
        others = [
            (lax.rem(row + down, rows), lax.rem(col + over, cols))
            for down in range(rows)
            for over in range(cols)
            if down or over
        ]

        weight_moves = [
            (wq_ref, "wqkv", 1, head_cols, 0),
            (wk_ref, "wqkv", 1, kv_cols, head_cols),
            (wv_ref, "wqkv", 1, kv_cols, head_cols + kv_cols),
            (wo_ref, "wo", 0, head_cols, 0),
            (wg_ref, "wgu", 1, ff, 0),
            (wu_ref, "wgu", 1, ff, ff),
            (wd_ref, "wd", 0, ff, 0),
        ]

        def weight_pair(move, owner):
            source, name, split, extent, start = move
            if split == 1:
                return (
                    source.at[:, :, at(owner, extent)],
                    ref[name].at[:, at(row, slab), pl.ds(start, extent)],
                )
            return (
                source.at[:, at(owner, extent), :],
                ref[name].at[:, :, at(row, slab)],
            )

        own_weights = {}
        for index, move in enumerate(weight_moves):
            source, target = weight_pair(move, row)
            copy = pltpu.make_async_copy(source, target, local.at[index])
            copy.start()
            own_weights.setdefault(move[1], []).append(copy)

        x0 = ref["x0"]
        gain = jnp.concatenate([again_ref[...], fgain_ref[...]], axis=0)
        high = gain.astype(BF)
        middle = (gain - high.astype(F32)).astype(BF)
        low = (gain - high.astype(F32) - middle.astype(F32)).astype(BF)
        zeros = jnp.zeros((16 - 3 * 2 * layers, block), BF)
        count = 2 * layers
        x0[me, pl.ds(0, tokens), :] = x_ref[...].astype(BF)
        x0[me, pl.ds(tokens, 16), :] = jnp.concatenate(
            [high[:count].astype(F32), middle[:count].astype(F32), low[:count].astype(F32),
             zeros.astype(F32)], axis=0
        ).astype(BF)

        barrier = pltpu.get_barrier_semaphore()
        greeted = [{"row": there[0], "col": there[1]} for there in others]
        greeted += [{"dp": lax.rem(place + step, dp)} for step in range(1, dp)]
        for peer in greeted:
            pl.semaphore_signal(barrier, inc=1, device_id=peer, device_id_type=MESH)
        pl.semaphore_wait(barrier, len(greeted))

        turns = {"gather": 0, "scatter": 0}

        def next_turn(kind):
            turns[kind] += 1
            return kind, turns[kind] % 2

        def gather_start(view, turn=None):
            turn = turn or next_turn("gather")
            mine = view(row, col)
            over = [None] * cols
            for step in range(cols - 1, 0, -1):
                over[step] = net.copy(
                    mine, mine, {"col": col_peers[step - 1]}, (*turn, "over", step)
                )
            down = [gather_down(mine, turn, 0)]
            return view, over, down, turn

        def gather_down(here, turn, step):
            return [
                net.copy(here, here, {"row": peer}, (*turn, "down", step, slot))
                for slot, peer in enumerate(row_peers)
            ]

        def gather_step(state, step):
            view, over, down, turn = state
            if step:
                over[step].wait_recv()
                here = view(row, lax.rem(col + cols - step, cols))
                down.append(gather_down(here, turn, step))

        def gather_rows(state, step):
            for copy in state[2][step]:
                copy.wait_recv()

        def gather_end(state):
            for copy in state[1][1:]:
                copy.wait_send()
            for line in state[2]:
                for copy in line:
                    copy.wait_send()

        def gather_rest(state):
            for step in range(1, cols):
                gather_step(state, step)
            for step in range(cols):
                gather_rows(state, step)
            gather_end(state)

        def chip_rows(source, target):
            parts = [source[at(there * cols + target, size), :] for there in range(rows)]
            return jnp.concatenate(parts, axis=0) if rows > 1 else parts[0]

        def store_rows(target_ref, target, value):
            for there in range(rows):
                target_ref[at(there * cols + target, size), :] = value[
                    there * size : (there + 1) * size
                ]

        part, mid = ref["part"], ref["mid"]

        def scatter(compute, order, fill_a=None, gather=None, slots=0, idle=None, between=None):
            first, second = {}, {}
            turn = next_turn("scatter")
            got_row, got_col = ref["got_row"].at[slots], ref["got_col"].at[slots]

            def pair_sum(step):
                target = lax.rem(col + cols - step, cols)
                total = part[at(row * cols + target, size), :].astype(F32)
                for slot in range(rows - 1):
                    first[slot, step].wait_recv()
                    total += got_row[slot, step].astype(F32)
                return total

            def forward(step):
                mid[step - 1] = pair_sum(step).astype(BF)
                target = lax.rem(col + cols - step, cols)
                second[step] = net.copy(
                    mid.at[step - 1], got_col.at[step - 1], {"col": target}, (*turn, "over", step)
                )

            waiting = []
            for step in order:
                target = lax.rem(col + cols - step, cols)
                if gather is not None:
                    gather_step(gather, step)
                    if step == cols - 1 and idle is not None:
                        idle()
                    gather_rows(gather, step)
                store_rows(part, target, compute(target).astype(BF))
                for slot, peer in enumerate(row_peers):
                    first[slot, step] = net.copy(
                        part.at[at(peer * cols + target, size), :],
                        got_row.at[slot, step],
                        {"row": peer},
                        (*turn, "down", step, slot),
                    )
                if waiting:
                    forward(waiting.pop())
                if step:
                    waiting.append(step)
            for step in waiting:
                forward(step)
            if gather is not None:
                gather_end(gather)
            if fill_a is not None:
                fill_a()
            total = pair_sum(0)
            if between is not None:
                between()
            for step in range(1, cols):
                second[step].wait_recv()
                total += got_col[step - 1].astype(F32)
            for copy in list(first.values()) + list(second.values()):
                copy.wait_send()
            return total

        late = list(range(1, cols)) + [0]
        early = list(range(cols))

        def feature_view(buffer):
            return lambda at_row, at_col: buffer.at[at_row * cols + at_col]

        def token_view(buffer):
            return lambda at_row, at_col: buffer.at[at(at_row * cols + at_col, size), :]

        first_gather = gather_start(feature_view(x0))

        sent_weights = {}

        def send_weights():
            for move in weight_moves:
                for peer in row_peers:
                    source, target = weight_pair(move, peer)
                    sent_weights.setdefault(move[1], []).append(
                        net.copy(source, target, {"row": peer})
                    )

        def need_weight(name):
            for copy in own_weights.pop(name, []):
                copy.wait()
            for copy in sent_weights.pop(name, []):
                copy.wait()

        def to_tokens(source, target):
            copies = []
            for there in others:
                index = there[0] * cols + there[1]
                copies.append(
                    net.copy(
                        source.at[at(index, size), :],
                        target.at[:, at(me, block)],
                        {"row": there[0], "col": there[1]},
                    )
                )
            target[:, at(me, block)] = source[at(me, size), :]
            return copies

        def to_features(source, target):
            copies = []
            for there in others:
                index = there[0] * cols + there[1]
                copies.append(
                    net.copy(
                        source.at[:, at(index, block)],
                        target.at[at(me, size), :],
                        {"row": there[0], "col": there[1]},
                    )
                )
            target[at(me, size), :] = source[:, at(me, block)]
            return copies

        send_weights()

        lane = lax.broadcasted_iota(jnp.int32, (128, HEAD_DIM), 1)
        low_half = lane < HEAD_DIM // 2
        exponent = jnp.where(low_half, lane, lane - HEAD_DIM // 2).astype(F32)
        inverse = jnp.exp2(exponent * (-2.0 * math.log2(rope_base) / HEAD_DIM))
        for index in range(tokens // 128):
            here = slice(index * 128, (index + 1) * 128)
            spot = jnp.broadcast_to(pos_ref[index : index + 1, :].astype(F32), (128, 128)).T
            angle = spot * inverse
            ref["cos"][here, :] = jnp.cos(angle)
            turn = jnp.sin(angle)
            ref["sin"][here, :] = jnp.where(low_half, -turn, turn)
            begin = index * 128 % SEQ_LEN
            for start in range(0, SEQ_LEN, 128):
                offset = (
                    begin - start
                    + lax.broadcasted_iota(jnp.int32, (128, 128), 0)
                    - lax.broadcasted_iota(jnp.int32, (128, 128), 1)
                ).astype(F32)
                seen = (offset >= 0.0) & (offset <= spot)
                ref["mask"][here, start : start + 128] = jnp.where(seen, 0.0, masked_score)

        gather_rest(first_gather)
        residual_moves = to_tokens(x_ref, ref["res"].at[0])

        gains = ref["gains"]
        for slot in range(group):
            split = x0[slot, pl.ds(tokens, 16), :].astype(F32)
            gains[0:count, slot * block : (slot + 1) * block] = (
                split[:count] + split[count : 2 * count] + split[2 * count : 3 * count]
            )

        for start in range(0, tokens, 128):
            length = pl.ds(start, 128)
            squares = jnp.zeros((128, block), F32)
            for slot in range(group):
                value = x0[slot, length, :].astype(F32)
                squares += value * value
            rate = lax.rsqrt(jnp.sum(squares, axis=1, keepdims=True) * (1.0 / width) + epsilon)
            for slot in range(group):
                lanes = slice(slot * block, (slot + 1) * block)
                ref["feat_a"][0, length, lanes] = (
                    x0[slot, length, :].astype(F32) * rate * gains[0:1, lanes]
                ).astype(BF)

        state = {}

        def attend(layer):
            raw, prep, att = (ref[k].at[layer] for k in ("raw", "prep", "att"))
            inv = ref["inv"]
            gain_q, gain_k = qgain_ref[layer : layer + 1], kgain_ref[layer : layer + 1]
            cosine, sine = cos_ref[...], sin_ref[...]
            for head in range(q_heads + kv_heads):
                lanes = slice(head * HEAD_DIM, (head + 1) * HEAD_DIM)
                gain_h = gain_q if head < q_heads else gain_k
                prep[:, lanes] = head_prepare(raw[:, lanes], gain_h, cosine, sine)
            for start in range(0, tokens, SEQ_LEN):
                for head in range(q_heads):
                    kv = head // members
                    k_lanes = slice(head_cols + kv * HEAD_DIM, head_cols + (kv + 1) * HEAD_DIM)
                    v_at = head_cols + kv_cols + kv * HEAD_DIM
                    v_lanes = slice(v_at, v_at + HEAD_DIM)
                    lanes = slice(head * HEAD_DIM, (head + 1) * HEAD_DIM)
                    for begin in range(0, SEQ_LEN, q_block):
                        mine = pl.ds(start + begin, q_block)
                        keys = pl.ds(start, begin + q_block)
                        scores = mm_t(prep[mine, lanes], prep[keys, k_lanes])
                        weights = jnp.exp2(
                            scores * (SCALE * LOG2E)
                            + ref["mask"][mine, 0 : begin + q_block]
                        )
                        inverse = 1.0 / jnp.sum(weights, axis=-1, keepdims=True)
                        lane = layer * q_heads + head
                        inv[mine, lane : lane + 1] = inverse
                        att[row, mine, lanes] = mm(
                            (weights * inverse).astype(BF), prep[keys, v_lanes]
                        ).astype(BF)

        def feature_block(value, gain_row, target):
            normed, rate = width_norm(value)
            target[at(me, size), :] = (normed * gains[gain_row : gain_row + 1, :]).astype(BF)

        def send_row(buffer):
            return [net.copy(buffer.at[row], buffer.at[row], {"row": peer}) for peer in row_peers]

        top_gathers = []
        top_parts = 4

        def top_start():
            extent = tokens // top_parts
            here = pl.ds(len(top_gathers) * extent, extent)
            top_gathers.append(
                gather_start(
                    lambda at_row, at_col: ref["t0"].at[at_row * cols + at_col, here, :],
                    ("top", len(top_gathers)),
                )
            )

        def top_forward(index):
            for step in range(1, cols):
                gather_step(top_gathers[index], step)

        ref["t0"][me] = og_ref[...].astype(BF)
        top_start()
        top_start()
        row_moves = {}
        last = layers - 1

        def feed_forward(layer, target):
            feat = chip_rows(ref["feat_f"].at[layer], target)
            both = mm(feat, ref["wgu"][layer])
            gate, up = both[:, :ff], both[:, ff:]
            sig = lax.logistic(gate)
            hidden = (gate * sig * up).astype(BF)
            store_rows(ref["hid"].at[layer, row], target, hidden)
            return both, gate, up, sig, hidden

        for layer in range(layers):
            feat_a, feat_f = ref["feat_a"].at[layer], ref["feat_f"].at[layer]
            raw = ref["raw"].at[layer]
            need_weight("wqkv")
            for start in range(0, tokens, 256):
                here = slice(start, start + 256)
                value = mm(feat_a[here, :], ref["wqkv"][layer])
                raw[here, :] = value[:, : head_cols + kv_cols]
                ref["prep"][layer, here, head_cols + kv_cols :] = value[
                    :, head_cols + kv_cols :
                ].astype(BF)
            attend(layer)
            need_weight("wo")

            def compute_o(target, layer=layer):
                return mm(chip_rows(ref["att"].at[layer, row], target), ref["wo"][layer])

            def during_o(layer=layer):
                row_moves["att", layer] = send_row(ref["att"].at[layer])
                if layer == last:
                    top_forward(3)

            total = scatter(compute_o, late, fill_a=during_o)
            if layer == 0:
                for copy in residual_moves:
                    copy.wait()
            ref["res"][2 * layer + 1] = ref["res"][2 * layer] + total
            feature_block(ref["res"][2 * layer + 1], layers + layer, feat_f)
            gathering = gather_start(token_view(feat_f))
            need_weight("wgu")
            need_weight("wd")
            if layer == last:
                break

            def compute_ff(target, layer=layer):
                both, gate, up, sig, hidden = feed_forward(layer, target)
                store_rows(ref["gu"].at[layer], target, both)
                return mm(hidden, ref["wd"][layer])

            def during_ff(layer=layer):
                row_moves["hid", layer] = send_row(ref["hid"].at[layer])

            def idle_ff(layer=layer):
                if layer == 0:
                    top_start()
                    top_forward(0)
                    top_forward(1)

            total = scatter(compute_ff, early, fill_a=during_ff, gather=gathering, idle=idle_ff)
            ref["res"][2 * layer + 2] = ref["res"][2 * layer + 1] + total
            feature_block(ref["res"][2 * layer + 2], layer + 1, ref["feat_a"].at[layer + 1])
            coming = gather_start(token_view(ref["feat_a"].at[layer + 1]))
            for step in range(1, cols):
                gather_step(coming, step)
            if layer == 0:
                top_start()
                top_forward(2)
                grad_moves = to_tokens(og_ref, ref["gtok"])
            for step in range(cols):
                gather_rows(coming, step)
            gather_end(coming)

        window = SUM_WINDOW
        half = dp // 2
        on_left = place < half
        depth = jnp.where(on_left, place, dp - 1 - place)
        inward = jnp.where(on_left, place + 1, place - 1)
        outward = jnp.where(on_left, place - 1, place + 1)
        outward = jnp.clip(outward, 0, dp - 1)
        is_mid = depth == half - 1
        inner = depth > 0

        def views(index):
            name, layer, start, extent = pieces[index]
            rows_at = pl.ds(start, extent)
            return (
                ref["acc_" + name].at[layer, rows_at, :],
                ref["frm_" + name].at[layer, rows_at, :],
                totals[name].at[layer, rows_at, :],
            )

        def hop(source, target, index, kind, peer):
            sems = {
                "up": (up_send, up_recv),
                "across": (up_send, in_recv),
                "back": (in_send, in_recv),
            }[kind]
            return pltpu.make_async_remote_copy(
                src_ref=source,
                dst_ref=target,
                send_sem=sems[0].at[index % window],
                recv_sem=sems[1].at[index],
                device_id={"dp": peer},
                device_id_type=MESH,
            )

        def send_inward(index, condition):
            acc, frm, tot = views(index)

            @pl.when(condition & jnp.logical_not(is_mid))
            def _():
                hop(acc, frm, index, "up", inward).start()

            @pl.when(condition & is_mid)
            def _():
                hop(acc, tot, index, "across", inward).start()

        def add_into(target, one, two):
            extent = one.shape[0]
            chunk = 32

            def body(step, carry):
                here = at(step, chunk)
                target[here, :] = (one[here, :].astype(F32) + two[here, :].astype(F32)).astype(BF)
                return carry

            lax.fori_loop(0, extent // chunk, body, 0)

        def sent_inward(index, condition):
            if index >= 0:
                acc, frm, tot = views(index)

                @pl.when(condition)
                def _():
                    hop(acc, frm, index, "up", inward).wait_send()

        def sent_outward(index, condition):
            if index >= 0:
                tot = views(index)[2]

                @pl.when(condition & inner)
                def _():
                    hop(tot, tot, index, "back", outward).wait_send()

        def up(index):
            sent_inward(index - window, jnp.logical_not(inner))
            send_inward(index, jnp.logical_not(inner))

        def across(index):
            acc, frm, tot = views(index)

            @pl.when(inner)
            def _():
                hop(acc, frm, index, "up", inward).wait_recv()
                add_into(acc, acc, frm)

            sent_inward(index - window, inner)
            send_inward(index, inner)

        def back(index):
            acc, frm, tot = views(index)

            @pl.when(is_mid)
            def _():
                hop(acc, tot, index, "across", inward).wait_recv()
                add_into(tot, acc, tot)

            sent_outward(index - window, is_mid)

            @pl.when(is_mid & inner)
            def _():
                hop(tot, tot, index, "back", outward).start()

        def outer(index):
            acc, frm, tot = views(index)

            @pl.when(jnp.logical_not(is_mid))
            def _():
                hop(tot, tot, index, "back", inward).wait_recv()

            sent_outward(index - window, jnp.logical_not(is_mid))

            @pl.when(jnp.logical_not(is_mid) & inner)
            def _():
                hop(tot, tot, index, "back", outward).start()

        done = {"made": 0, "up": 0, "across": 0, "back": 0}
        ahead_up, ahead_across = 3, 2

        def made(count_new):
            done["made"] += count_new

        def advance(name, action):
            action(done[name])
            done[name] += 1

        def pump(count_steps=1):
            for _ in range(count_steps):
                if done["up"] < done["made"]:
                    advance("up", up)
                    if done["across"] < done["up"] - ahead_up:
                        advance("across", across)
                    if done["back"] < done["across"] - ahead_across:
                        advance("back", back)

        def finish():
            while done["back"] < n_pieces:
                if done["up"] < n_pieces:
                    advance("up", up)
                for _ in range(2):
                    if done["across"] < min(n_pieces, done["up"] - 1 + done["up"] // n_pieces):
                        advance("across", across)
                for _ in range(2):
                    if done["back"] < min(n_pieces, done["across"] - 1 + done["across"] // n_pieces):
                        advance("back", back)
            stores = []
            for index in range(n_pieces):
                outer(index)
                name, layer, start, extent = pieces[index]
                if index + 1 < n_pieces and pieces[index + 1][:2] == (name, layer):
                    continue
                copy = pltpu.make_async_copy(
                    totals[name].at[layer], results[name].at[layer], stored.at[len(stores)]
                )
                copy.start()
                stores.append(copy)
            for copy in stores:
                copy.wait()
            for index in range(n_pieces - window, n_pieces):
                sent_inward(index, depth >= 0)
                sent_outward(index, depth >= 0)

        gb, gb2 = ref["gb"].at[0], ref["gb"].at[1]
        for index in range(top_parts):
            for step in range(cols):
                gather_rows(top_gathers[index], step)
            gather_end(top_gathers[index])
        for slot in range(group):
            gb[:, slot * block : (slot + 1) * block] = ref["t0"][slot]
        gtok, sums = ref["gtok"], ref["sums"]
        for slot in range(group):
            sums[slot] = jnp.zeros((16, HEAD_DIM), F32)

        def slab_of(source):
            return source[:, at(row, slab)]

        quarter = slab // 4

        def slab_part(source, index):
            start = pl.multiple_of(row * slab + index * quarter, quarter)
            return source[:, pl.ds(start, quarter)]

        def norm_back(total, residual, gain_row):
            normed, rate = width_norm(residual)
            scaled = total * gains[gain_row : gain_row + 1, :]
            inner_mean = jnp.mean(scaled * normed, axis=1, keepdims=True)
            gtok[...] = gtok[...] + rate * (scaled - normed * inner_mean)
            line = jnp.sum(total * normed, axis=0, keepdims=True)
            for slot in range(group):
                sums[slot, gain_row : gain_row + 1, :] = line[:, slot * block : (slot + 1) * block]

        def attend_back(layer):
            raw, prep, att = (ref[k].at[layer] for k in ("raw", "prep", "att"))
            inv = ref["inv"]
            gain_q, gain_k = qgain_ref[layer : layer + 1], kgain_ref[layer : layer + 1]
            dqkv, datt = ref["dqkv"], ref["datt"]
            dk, dv, dq = ref["dkv"].at[0], ref["dkv"].at[1], ref["dq"]
            cosine, sine = cos_ref[...], sin_ref[...]
            total_q = jnp.zeros((1, HEAD_DIM), F32)
            total_k = jnp.zeros((1, HEAD_DIM), F32)
            for kv in range(kv_heads):
                k_lanes = slice(head_cols + kv * HEAD_DIM, head_cols + (kv + 1) * HEAD_DIM)
                v_at = head_cols + kv_cols + kv * HEAD_DIM
                v_lanes = slice(v_at, v_at + HEAD_DIM)
                dk[...] = jnp.zeros((tokens, HEAD_DIM), F32)
                dv[...] = jnp.zeros((tokens, HEAD_DIM), F32)
                for member in range(members):
                    head = kv * members + member
                    lanes = slice(head * HEAD_DIM, (head + 1) * HEAD_DIM)
                    lane = layer * q_heads + head
                    for start in range(0, tokens, SEQ_LEN):
                        for begin in range(0, SEQ_LEN, q_block):
                            mine = pl.ds(start + begin, q_block)
                            keys = pl.ds(start, begin + q_block)
                            scores = mm_t(prep[mine, lanes], prep[keys, k_lanes])
                            probs = jnp.exp2(
                                scores * (SCALE * LOG2E)
                                + ref["mask"][mine, 0 : begin + q_block]
                            ) * inv[mine, lane : lane + 1]
                            grad_o = datt[mine, lanes]
                            inner_sum = jnp.sum(
                                grad_o.astype(F32) * att[row, mine, lanes].astype(F32),
                                axis=-1,
                                keepdims=True,
                            )
                            dv[keys, :] += t_mm(probs.astype(BF), grad_o)
                            grad_s = (
                                probs * (mm_t(grad_o, prep[keys, v_lanes]) - inner_sum)
                            ).astype(BF)
                            dq[mine, :] = mm(grad_s, prep[keys, k_lanes]) * SCALE
                            dk[keys, :] += t_mm(grad_s, prep[mine, lanes])
                    back, line = head_back(dq[...], raw[:, lanes], gain_q, cosine, sine)
                    dqkv[row, :, lanes] = back.astype(BF)
                    total_q += line
                back, line = head_back(dk[...] * SCALE, raw[:, k_lanes], gain_k, cosine, sine)
                dqkv[row, :, k_lanes] = back.astype(BF)
                dqkv[row, :, v_lanes] = dv[...].astype(BF)
                total_k += line
            at_row = 8 + 2 * layer
            for slot in range(group):
                sums[slot, at_row : at_row + 1, :] = total_q
                sums[slot, at_row + 1 : at_row + 2, :] = total_k

        for layer in reversed(range(layers)):
            feat_a, feat_f = ref["feat_a"].at[layer], ref["feat_f"].at[layer]
            if layer != last:
                gb[at(me, size), :] = gtok[...].astype(BF)
                gathering = gather_start(token_view(gb))

            def compute_ff_back(target, layer=layer):
                grad = chip_rows(gb, target)
                if layer == last:
                    both, gate, up, sig, hidden = feed_forward(layer, target)
                else:
                    both = chip_rows(ref["gu"].at[layer], target)
                    gate, up = both[:, :ff], both[:, ff:]
                    sig = lax.logistic(gate)
                dhid = mm_t(grad, ref["wd"][layer])
                dgate = (dhid * up * sig * (1.0 + gate * (1.0 - sig))).astype(BF)
                dup = (dhid * gate * sig).astype(BF)
                joined = jnp.concatenate([dgate, dup], axis=1)
                store_rows(ref["dgu"].at[row], target, joined)
                return mm_t(joined, ref["wgu"][layer])

            def ffn_grads(layer=layer, feat_f=feat_f):
                if layer == last:
                    row_moves["hid", layer] = send_row(ref["hid"].at[layer])
                moves = send_row(ref["dgu"])
                for copy in row_moves.pop(("hid", layer)):
                    copy.wait()
                right = slab_of(gb)
                for there in range(rows):
                    ref["acc_down"][layer, there * ff : (there + 1) * ff, :] = t_mm(
                        ref["hid"][layer, there], right
                    ).astype(BF)
                made(2)
                pump(2)
                for copy in moves:
                    copy.wait()
                for index in range(4):
                    left = slab_part(feat_f, index)
                    here = slice(index * quarter, (index + 1) * quarter)
                    for there in range(rows):
                        value = t_mm(left, ref["dgu"][there]).astype(BF)
                        ref["acc_gu"][layer, here, there * ff : (there + 1) * ff] = value[:, :ff]
                        begin = (rows + there) * ff
                        ref["acc_gu"][layer, here, begin : begin + ff] = value[:, ff:]
                made(4)
                pump()

            total = scatter(
                compute_ff_back, early, fill_a=ffn_grads, gather=gathering, idle=pump, between=pump
            )
            if layer == last:
                for copy in grad_moves:
                    copy.wait()
            norm_back(total, ref["res"][2 * layer + 1], layers + layer)
            gb2[at(me, size), :] = gtok[...].astype(BF)
            gathering = gather_start(token_view(gb2))
            pump()
            gather_rest(gathering)
            pump()
            for start in range(0, tokens, 256):
                ref["datt"][start : start + 256, :] = mm_t(
                    gb2[start : start + 256, :], ref["wo"][layer]
                ).astype(BF)
            attend_back(layer)
            pump()
            moves = send_row(ref["dqkv"])

            def compute_qkv_back(target, layer=layer):
                return mm_t(chip_rows(ref["dqkv"].at[row], target), ref["wqkv"][layer])

            def attn_grads(layer=layer, feat_a=feat_a, moves=moves):
                for copy in row_moves.pop(("att", layer)):
                    copy.wait()
                right = slab_of(gb2)
                for there in range(rows):
                    ref["acc_o"][layer, there * head_cols : (there + 1) * head_cols, :] = t_mm(
                        ref["att"][layer, there], right
                    ).astype(BF)
                made(2)
                pump()
                for copy in moves:
                    copy.wait()
                acc = ref["acc_qkv"]
                for index in range(4):
                    left = slab_part(feat_a, index)
                    here = slice(index * quarter, (index + 1) * quarter)
                    for there in range(rows):
                        value = t_mm(left, ref["dqkv"][there]).astype(BF)
                        begin = there * head_cols
                        acc[layer, here, begin : begin + head_cols] = value[:, :head_cols]
                        begin = rows * head_cols + there * kv_cols
                        acc[layer, here, begin : begin + kv_cols] = value[
                            :, head_cols : head_cols + kv_cols
                        ]
                        begin += rows * kv_cols
                        acc[layer, here, begin : begin + kv_cols] = value[:, head_cols + kv_cols :]
                made(4)
                pump()

            total = scatter(compute_qkv_back, late, fill_a=attn_grads, between=pump)
            norm_back(total, ref["res"][2 * layer], layer)
            pump()

        sums_in, dsum = ref["sums_in"], ref["dsum"]
        sum_moves = []
        for there in others:
            index = there[0] * cols + there[1]
            sum_moves.append(
                net.copy(sums.at[index], sums_in.at[me], {"row": there[0], "col": there[1]})
            )
        sums_in[me] = sums[me]
        din_moves = to_features(gtok, din_ref)

        def compute_down(target):
            return mm(chip_rows(ref["hid"].at[last, row], target), ref["wd"][last])

        pump()
        result = scatter(compute_down, late, slots=1)
        ref["fin"][...] = ref["res"][2 * last + 1] + result
        out_moves = to_features(ref["fin"], out_ref)
        for copy in sum_moves:
            copy.wait()
        total = sums_in[0]
        for slot in range(1, group):
            total += sums_in[slot]
        dsum[place] = total
        sum_moves = [
            net.copy(dsum.at[place], dsum.at[place], {"dp": lax.rem(place + step, dp)})
            for step in range(1, dp)
        ]
        for copy in din_moves + out_moves:
            copy.wait()
        for copy in sum_moves:
            copy.wait()
        total = dsum[0]
        for slot in range(1, dp):
            total += dsum[slot]
        small_ref[...] = total
        finish()

    def call(*operands):
        shapes_out = [
            jax.ShapeDtypeStruct((tokens, block), F32),
            jax.ShapeDtypeStruct((tokens, block), F32),
            jax.ShapeDtypeStruct((16, HEAD_DIM), F32),
        ] + [jax.ShapeDtypeStruct(grad_shapes[name], BF) for name in grad_names]
        return pl.pallas_call(
            kernel,
            name="layers",
            out_shape=shapes_out,
            in_specs=[VM] * 7 + [ANY] * 7,
            out_specs=[VM] * 3 + [ANY] * len(grad_names),
            scratch_shapes=[pltpu.VMEM(*scratch[name]) for name in names]
            + [
                pltpu.SemaphoreType.DMA((limit,)),
                pltpu.SemaphoreType.DMA((limit,)),
                pltpu.SemaphoreType.DMA((7,)),
            ]
            + [
                pltpu.SemaphoreType.DMA((extent,))
                for extent in (
                    SUM_WINDOW, n_pieces, SUM_WINDOW, n_pieces, len(grad_names) * layers,
                )
            ],
            compiler_params=pltpu.CompilerParams(
                collective_id=1, has_side_effects=True, vmem_limit_bytes=60 << 20
            ),
        )(*operands)

    return call


def per_device(
    sizes,
    residual_in,
    positions,
    attn_gain,
    query_weight,
    key_weight,
    value_weight,
    query_gain,
    key_gain,
    output_weight,
    ffn_gain,
    gate_weight,
    up_weight,
    down_weight,
    output_grad,
):
    dp, rows, cols = sizes
    layers = query_weight.shape[0]
    tokens, block = residual_in.shape
    shapes = (
        layers, tokens, block, query_weight.shape[2] // rows, key_weight.shape[2] // rows,
        gate_weight.shape[2] // rows,
    )
    outputs, input_grad, small, down, gu, out_w, qkv = layers_kernel(sizes, shapes)(
        residual_in, output_grad, attn_gain, ffn_gain, query_gain, key_gain,
        positions.reshape(tokens // 128, 128),
        query_weight, key_weight, value_weight, output_weight, gate_weight, up_weight, down_weight,
    )
    return widen(
        outputs, input_grad, small, down, gu, out_w, qkv,
        (query_weight.shape[2], key_weight.shape[2], gate_weight.shape[2]),
    )


def widen(outputs, input_grad, small, down, gu, out_w, qkv, columns):
    wide_q, wide_k, wide_f = columns
    layers, parts = down.shape[0], 2
    tokens, block = outputs.shape

    def kernel(
        out_in, din_in, small_in, down_in, gu_in, o_in, qkv_in,
        out_ref, din_ref, again_ref, q_ref, k_ref, v_ref, qgain_ref, kgain_ref, o_ref, fgain_ref,
        gate_ref, up_ref, down_ref,
    ):
        out_ref[...] = out_in[...]
        din_ref[...] = din_in[...]
        again_ref[...] = small_in[0:layers, :]
        fgain_ref[...] = small_in[layers : 2 * layers, :]
        for layer in range(layers):
            start = 8 + 2 * layer
            qgain_ref[layer : layer + 1, :] = small_in[start : start + 1, :]
            kgain_ref[layer : layer + 1, :] = small_in[start + 1 : start + 2, :]
        q_ref[...] = qkv_in[:, :, :wide_q].astype(F32)
        k_ref[...] = qkv_in[:, :, wide_q : wide_q + wide_k].astype(F32)
        v_ref[...] = qkv_in[:, :, wide_q + wide_k :].astype(F32)
        o_ref[...] = o_in[...].astype(F32)
        gate_ref[...] = gu_in[:, :, :wide_f].astype(F32)
        up_ref[...] = gu_in[:, :, wide_f:].astype(F32)
        down_ref[...] = down_in[...].astype(F32)

    flat = pl.BlockSpec((tokens // (layers * parts), block), lambda i, j: (i * parts + j, 0))

    def whole(shape):
        return pl.BlockSpec(shape, lambda i, j: (0,) * len(shape))

    def cut(height, width):
        return pl.BlockSpec((1, height // parts, width), lambda i, j: (i, j, 0))

    def shape_of(*extent):
        return jax.ShapeDtypeStruct(extent, F32)

    slab, wide_d = qkv.shape[1], down.shape[1]
    wide_o, out_cols = out_w.shape[1:]
    gain = (layers, block)
    head_gain = (layers, HEAD_DIM)
    return pl.pallas_call(
        kernel,
        name="widen",
        grid=(layers, parts),
        in_specs=[
            flat, flat, whole(small.shape), cut(wide_d, out_cols), cut(slab, gu.shape[2]),
            cut(wide_o, out_cols), cut(slab, qkv.shape[2]),
        ],
        out_specs=[
            flat, flat, whole(gain), cut(slab, wide_q), cut(slab, wide_k), cut(slab, wide_k),
            whole(head_gain), whole(head_gain), cut(wide_o, out_cols), whole(gain),
            cut(slab, wide_f), cut(slab, wide_f), cut(wide_d, out_cols),
        ],
        out_shape=[
            shape_of(tokens, block), shape_of(tokens, block), shape_of(*gain),
            shape_of(layers, slab, wide_q), shape_of(layers, slab, wide_k),
            shape_of(layers, slab, wide_k), shape_of(*head_gain), shape_of(*head_gain),
            shape_of(layers, wide_o, out_cols), shape_of(*gain),
            shape_of(layers, slab, wide_f), shape_of(layers, slab, wide_f),
            shape_of(layers, wide_d, out_cols),
        ],
        compiler_params=pltpu.CompilerParams(vmem_limit_bytes=60 << 20),
    )(outputs, input_grad, small, down, gu, out_w, qkv)


def solution(mesh):
    wide = P("dp", ("row", "col"))
    gain = P(None, ("row", "col"))
    into, out_of = P(None, "row", "col"), P(None, "col", "row")
    in_specs = (
        wide, P("dp"), gain, into, into, into, P(), P(), out_of, gain, into, into, out_of, wide,
    )
    out_specs = (wide, wide, gain, into, into, into, P(), P(), out_of, gain, into, into, out_of)
    return jax.shard_map(
        functools.partial(per_device, (mesh.shape["dp"], mesh.shape["row"], mesh.shape["col"])),
        mesh=mesh,
        in_specs=in_specs,
        out_specs=out_specs,
        check_vma=False,
    )
```

```python
import functools
import math

import jax
import jax.numpy as jnp
from jax import lax
from jax.experimental import pallas as pl
from jax.experimental.pallas import tpu as pltpu
from jax.sharding import PartitionSpec as P

HEAD_DIM = 128
SEQ_LEN = 512

SUM_WINDOW = 3
epsilon = 1e-06
rope_base = 1000000.0
masked_score = -1e30
MESH = pl.DeviceIdType.MESH
BF = jnp.bfloat16
F32 = jnp.float32
SCALE = HEAD_DIM ** (-0.5)
LOG2E = math.log2(math.e)
VM = pl.BlockSpec(memory_space=pltpu.VMEM)
ANY = pl.BlockSpec(memory_space=pl.ANY)


def dot(left, right, dims):
    return lax.dot_general(left, right, (dims, ((), ())), preferred_element_type=F32)


def mm(left, right):
    return dot(left, right, ((1,), (0,)))


def mm_t(left, right):
    return dot(left, right, ((1,), (1,)))


def t_mm(left, right):
    return dot(left, right, ((0,), (0,)))


def at(index, size):
    return pl.ds(pl.multiple_of(index * size, size), size)


def half_turn(values):
    return pltpu.roll(values, HEAD_DIM // 2, 1)


def head_norm(values):
    scaling = lax.rsqrt(jnp.mean(values * values, axis=-1, keepdims=True) + epsilon)
    return values * scaling, scaling


def head_prepare(values, gain, cosine, sine):
    normed = head_norm(values)[0] * gain
    return (normed * cosine + half_turn(normed) * sine).astype(BF)


def head_back(grad, values, gain, cosine, sine):
    normed, scaling = head_norm(values)
    turned = grad * cosine + half_turn(grad * sine)
    scaled = turned * gain
    inner = jnp.mean(scaled * normed, axis=-1, keepdims=True)
    return (
        scaling * (scaled - normed * inner),
        jnp.sum(turned * normed, axis=0, keepdims=True),
    )


def width_norm(residual):
    rate = lax.rsqrt(jnp.mean(residual * residual, axis=1, keepdims=True) + epsilon)
    return residual * rate, rate


class Net:
    def __init__(self, send, recv, limit):
        self.send, self.recv, self.limit, self.used = send, recv, limit, {}

    def copy(self, source, target, device, key=None):
        index = self.used.setdefault(len(self.used) if key is None else key, len(self.used))
        assert index < self.limit
        made = pltpu.make_async_remote_copy(
            src_ref=source,
            dst_ref=target,
            send_sem=self.send.at[index],
            recv_sem=self.recv.at[index],
            device_id=device,
            device_id_type=MESH,
        )
        made.start()
        return made


def layers_kernel(sizes, shapes):
    dp, rows, cols = sizes
    group = rows * cols
    layers, tokens, block, head_cols, kv_cols, ff = shapes
    width = block * group
    slab = width // rows
    size = tokens // group
    q_heads, kv_heads = head_cols // HEAD_DIM, kv_cols // HEAD_DIM
    members = q_heads // kv_heads
    qkv_cols = head_cols + 2 * kv_cols
    q_block = min(SEQ_LEN, 256)
    limit = 107 + dp
    chip = rows * size

    pieces = []
    for layer in reversed(range(layers)):
        for name, extent, parts in (
            ("down", rows * ff, 2), ("gu", slab, 4), ("o", rows * head_cols, 2), ("qkv", slab, 4),
        ):
            for part in range(parts):
                pieces.append((name, layer, part * extent // parts, extent // parts))
    n_pieces = len(pieces)

    grad_shapes = {
        "down": (layers, rows * ff, slab),
        "gu": (layers, slab, 2 * rows * ff),
        "o": (layers, rows * head_cols, slab),
        "qkv": (layers, slab, rows * qkv_cols),
    }
    grad_names = list(grad_shapes)

    scratch = {
        "x0": ((group, tokens + 16, block), BF),
        "t0": ((group, tokens, block), BF),
        "fin": ((size, width), F32),
        "gains": ((8, width), F32),
        "mask": ((tokens, SEQ_LEN), F32),
        "wqkv": ((layers, width, qkv_cols), BF),
        "wo": ((layers, head_cols, width), BF),
        "wgu": ((layers, width, 2 * ff), BF),
        "wd": ((layers, ff, width), BF),
        "feat_a": ((layers, tokens, width), BF),
        "feat_f": ((layers, tokens, width), BF),
        "res": ((2 * layers, size, width), F32),
        "raw": ((layers, tokens, head_cols + kv_cols), F32),
        "prep": ((layers, tokens, qkv_cols), BF),
        "inv": ((tokens, HEAD_DIM), F32),
        "att": ((layers, rows, tokens, head_cols), BF),
        "gu": ((max(layers - 1, 1), tokens, 2 * ff), F32),
        "cos": ((tokens, HEAD_DIM), F32),
        "sin": ((tokens, HEAD_DIM), F32),
        "hid": ((layers, rows, tokens, ff), BF),
        "part": ((tokens, width), BF),
        "got_row": ((2, max(rows - 1, 1), cols, size, width), BF),
        "mid": ((max(cols - 1, 1), size, width), BF),
        "got_col": ((2, max(cols - 1, 1), size, width), BF),
        "gb": ((2, tokens, width), BF),
        "dgu": ((rows, tokens, 2 * ff), BF),
        "dqkv": ((rows, tokens, qkv_cols), BF),
        "datt": ((tokens, head_cols), BF),
        "dkv": ((2, tokens, HEAD_DIM), F32),
        "dq": ((tokens, HEAD_DIM), F32),
        "gtok": ((size, width), F32),
        "sums": ((group, 16, HEAD_DIM), F32),
        "sums_in": ((group, 16, HEAD_DIM), F32),
        "dsum": ((dp, 16, HEAD_DIM), F32),
    }
    for name in grad_names:
        scratch["acc_" + name] = (grad_shapes[name], BF)
        scratch["frm_" + name] = (grad_shapes[name], BF)
        scratch["tot_" + name] = (grad_shapes[name], BF)
    names = list(scratch)

    def kernel(
        x_ref, og_ref, again_ref, fgain_ref, qgain_ref, kgain_ref, pos_ref,
        wq_ref, wk_ref, wv_ref, wo_ref, wg_ref, wu_ref, wd_ref,
        out_ref, din_ref, small_ref, t_down, t_gu, t_o, t_qkv, *rest,
    ):
        ref = dict(zip(names, rest))
        send, recv, local, up_send, up_recv, in_send, in_recv, stored = rest[len(names):]
        totals = {name: ref["tot_" + name] for name in grad_names}
        results = dict(zip(grad_names, (t_down, t_gu, t_o, t_qkv)))
        cos_ref, sin_ref = ref["cos"], ref["sin"]
        net = Net(send, recv, limit)
        row, col, place = lax.axis_index("row"), lax.axis_index("col"), lax.axis_index("dp")
        me = row * cols + col
        row_peers = [lax.rem(row + step, rows) for step in range(1, rows)]
        col_peers = [lax.rem(col + step, cols) for step in range(1, cols)]
        others = [
            (lax.rem(row + down, rows), lax.rem(col + over, cols))
            for down in range(rows)
            for over in range(cols)
            if down or over
        ]

        weight_moves = [
            (wq_ref, "wqkv", 1, head_cols, 0),
            (wk_ref, "wqkv", 1, kv_cols, head_cols),
            (wv_ref, "wqkv", 1, kv_cols, head_cols + kv_cols),
            (wo_ref, "wo", 0, head_cols, 0),
            (wg_ref, "wgu", 1, ff, 0),
            (wu_ref, "wgu", 1, ff, ff),
            (wd_ref, "wd", 0, ff, 0),
        ]

        def weight_pair(move, owner):
            source, name, split, extent, start = move
            if split == 1:
                return (
                    source.at[:, :, at(owner, extent)],
                    ref[name].at[:, at(row, slab), pl.ds(start, extent)],
                )
            return (
                source.at[:, at(owner, extent), :],
                ref[name].at[:, :, at(row, slab)],
            )

        own_weights = {}
        for index, move in enumerate(weight_moves):
            source, target = weight_pair(move, row)
            copy = pltpu.make_async_copy(source, target, local.at[index])
            copy.start()
            own_weights.setdefault(move[1], []).append(copy)

        x0 = ref["x0"]
        gain = jnp.concatenate([again_ref[...], fgain_ref[...]], axis=0)
        high = gain.astype(BF)
        middle = (gain - high.astype(F32)).astype(BF)
        low = (gain - high.astype(F32) - middle.astype(F32)).astype(BF)
        zeros = jnp.zeros((16 - 3 * 2 * layers, block), BF)
        count = 2 * layers
        x0[me, pl.ds(0, tokens), :] = x_ref[...].astype(BF)
        x0[me, pl.ds(tokens, 16), :] = jnp.concatenate(
            [high[:count].astype(F32), middle[:count].astype(F32), low[:count].astype(F32),
             zeros.astype(F32)], axis=0
        ).astype(BF)

        barrier = pltpu.get_barrier_semaphore()
        greeted = [{"row": there[0], "col": there[1]} for there in others]
        greeted += [{"dp": lax.rem(place + step, dp)} for step in range(1, dp)]
        for peer in greeted:
            pl.semaphore_signal(barrier, inc=1, device_id=peer, device_id_type=MESH)
        pl.semaphore_wait(barrier, len(greeted))

        turns = {"gather": 0, "scatter": 0}

        def next_turn(kind):
            turns[kind] += 1
            return kind, turns[kind] % 2

        def gather_start(view, turn=None):
            turn = turn or next_turn("gather")
            mine = view(row, col)
            over = [None] * cols
            for step in range(cols - 1, 0, -1):
                over[step] = net.copy(
                    mine, mine, {"col": col_peers[step - 1]}, (*turn, "over", step)
                )
            down = [gather_down(mine, turn, 0)]
            return view, over, down, turn

        def gather_down(here, turn, step):
            return [
                net.copy(here, here, {"row": peer}, (*turn, "down", step, slot))
                for slot, peer in enumerate(row_peers)
            ]

        def gather_step(state, step):
            view, over, down, turn = state
            if step:
                over[step].wait_recv()
                here = view(row, lax.rem(col + cols - step, cols))
                down.append(gather_down(here, turn, step))

        def gather_rows(state, step):
            for copy in state[2][step]:
                copy.wait_recv()

        def gather_end(state):
            for copy in state[1][1:]:
                copy.wait_send()
            for line in state[2]:
                for copy in line:
                    copy.wait_send()

        def gather_rest(state):
            for step in range(1, cols):
                gather_step(state, step)
            for step in range(cols):
                gather_rows(state, step)
            gather_end(state)

        def chip_rows(source, target):
            parts = [source[at(there * cols + target, size), :] for there in range(rows)]
            return jnp.concatenate(parts, axis=0) if rows > 1 else parts[0]

        def store_rows(target_ref, target, value):
            for there in range(rows):
                target_ref[at(there * cols + target, size), :] = value[
                    there * size : (there + 1) * size
                ]

        part, mid = ref["part"], ref["mid"]

        def scatter(compute, order, fill_a=None, gather=None, slots=0, idle=None, between=None, begin=None):
            first, second = {}, {}
            turn = next_turn("scatter")
            got_row, got_col = ref["got_row"].at[slots], ref["got_col"].at[slots]

            def pair_sum(step):
                target = lax.rem(col + cols - step, cols)
                total = part[at(row * cols + target, size), :].astype(F32)
                for slot in range(rows - 1):
                    first[slot, step].wait_recv()
                    total += got_row[slot, step].astype(F32)
                return total

            def forward(step):
                mid[step - 1] = pair_sum(step).astype(BF)
                target = lax.rem(col + cols - step, cols)
                second[step] = net.copy(
                    mid.at[step - 1], got_col.at[step - 1], {"col": target}, (*turn, "over", step)
                )

            waiting = []
            for step in order:
                target = lax.rem(col + cols - step, cols)
                if gather is not None:
                    gather_step(gather, step)
                    if step == cols - 1 and idle is not None:
                        idle()
                    gather_rows(gather, step)
                store_rows(part, target, compute(target).astype(BF))
                for slot, peer in enumerate(row_peers):
                    first[slot, step] = net.copy(
                        part.at[at(peer * cols + target, size), :],
                        got_row.at[slot, step],
                        {"row": peer},
                        (*turn, "down", step, slot),
                    )
                if waiting:
                    forward(waiting.pop())
                if step:
                    waiting.append(step)
            if begin is not None:
                begin()
            for step in waiting:
                forward(step)
            if gather is not None:
                gather_end(gather)
            if fill_a is not None:
                fill_a()
            total = pair_sum(0)
            if between is not None:
                between()
            for step in range(1, cols):
                second[step].wait_recv()
                total += got_col[step - 1].astype(F32)
            for copy in list(first.values()) + list(second.values()):
                copy.wait_send()
            return total

        late = list(range(1, cols)) + [0]
        early = list(range(cols))

        def feature_view(buffer):
            return lambda at_row, at_col: buffer.at[at_row * cols + at_col]

        def token_view(buffer):
            return lambda at_row, at_col: buffer.at[at(at_row * cols + at_col, size), :]

        first_gather = gather_start(feature_view(x0))

        sent_weights = {}

        def send_weights():
            for move in weight_moves:
                for peer in row_peers:
                    source, target = weight_pair(move, peer)
                    sent_weights.setdefault(move[1], []).append(
                        net.copy(source, target, {"row": peer})
                    )

        def need_weight(name):
            for copy in own_weights.pop(name, []):
                copy.wait()
            for copy in sent_weights.pop(name, []):
                copy.wait()

        def to_tokens(source, target):
            copies = []
            for there in others:
                index = there[0] * cols + there[1]
                copies.append(
                    net.copy(
                        source.at[at(index, size), :],
                        target.at[:, at(me, block)],
                        {"row": there[0], "col": there[1]},
                    )
                )
            target[:, at(me, block)] = source[at(me, size), :]
            return copies

        def to_features(source, target):
            copies = []
            for there in others:
                index = there[0] * cols + there[1]
                copies.append(
                    net.copy(
                        source.at[:, at(index, block)],
                        target.at[at(me, size), :],
                        {"row": there[0], "col": there[1]},
                    )
                )
            target[at(me, size), :] = source[:, at(me, block)]
            return copies

        send_weights()

        lane = lax.broadcasted_iota(jnp.int32, (128, HEAD_DIM), 1)
        low_half = lane < HEAD_DIM // 2
        exponent = jnp.where(low_half, lane, lane - HEAD_DIM // 2).astype(F32)
        inverse = jnp.exp2(exponent * (-2.0 * math.log2(rope_base) / HEAD_DIM))
        for index in range(tokens // 128):
            here = slice(index * 128, (index + 1) * 128)
            spot = jnp.broadcast_to(pos_ref[index : index + 1, :].astype(F32), (128, 128)).T
            angle = spot * inverse
            ref["cos"][here, :] = jnp.cos(angle)
            turn = jnp.sin(angle)
            ref["sin"][here, :] = jnp.where(low_half, -turn, turn)
            begin = index * 128 % SEQ_LEN
            for start in range(0, SEQ_LEN, 128):
                offset = (
                    begin - start
                    + lax.broadcasted_iota(jnp.int32, (128, 128), 0)
                    - lax.broadcasted_iota(jnp.int32, (128, 128), 1)
                ).astype(F32)
                seen = (offset >= 0.0) & (offset <= spot)
                ref["mask"][here, start : start + 128] = jnp.where(seen, 0.0, masked_score)

        gather_rest(first_gather)
        residual_moves = to_tokens(x_ref, ref["res"].at[0])

        gains = ref["gains"]
        for slot in range(group):
            split = x0[slot, pl.ds(tokens, 16), :].astype(F32)
            gains[0:count, slot * block : (slot + 1) * block] = (
                split[:count] + split[count : 2 * count] + split[2 * count : 3 * count]
            )

        for start in range(0, tokens, 128):
            length = pl.ds(start, 128)
            squares = jnp.zeros((128, block), F32)
            for slot in range(group):
                value = x0[slot, length, :].astype(F32)
                squares += value * value
            rate = lax.rsqrt(jnp.sum(squares, axis=1, keepdims=True) * (1.0 / width) + epsilon)
            for slot in range(group):
                lanes = slice(slot * block, (slot + 1) * block)
                ref["feat_a"][0, length, lanes] = (
                    x0[slot, length, :].astype(F32) * rate * gains[0:1, lanes]
                ).astype(BF)

        state = {}

        def attend(layer):
            raw, prep, att = (ref[k].at[layer] for k in ("raw", "prep", "att"))
            inv = ref["inv"]
            gain_q, gain_k = qgain_ref[layer : layer + 1], kgain_ref[layer : layer + 1]
            cosine, sine = cos_ref[...], sin_ref[...]
            for head in range(q_heads + kv_heads):
                lanes = slice(head * HEAD_DIM, (head + 1) * HEAD_DIM)
                gain_h = gain_q if head < q_heads else gain_k
                prep[:, lanes] = head_prepare(raw[:, lanes], gain_h, cosine, sine)
            for start in range(0, tokens, SEQ_LEN):
                for head in range(q_heads):
                    kv = head // members
                    k_lanes = slice(head_cols + kv * HEAD_DIM, head_cols + (kv + 1) * HEAD_DIM)
                    v_at = head_cols + kv_cols + kv * HEAD_DIM
                    v_lanes = slice(v_at, v_at + HEAD_DIM)
                    lanes = slice(head * HEAD_DIM, (head + 1) * HEAD_DIM)
                    for begin in range(0, SEQ_LEN, q_block):
                        mine = pl.ds(start + begin, q_block)
                        keys = pl.ds(start, begin + q_block)
                        scores = mm_t(prep[mine, lanes], prep[keys, k_lanes])
                        weights = jnp.exp2(
                            scores * (SCALE * LOG2E)
                            + ref["mask"][mine, 0 : begin + q_block]
                        )
                        inverse = 1.0 / jnp.sum(weights, axis=-1, keepdims=True)
                        lane = layer * q_heads + head
                        inv[mine, lane : lane + 1] = inverse
                        att[row, mine, lanes] = mm(
                            (weights * inverse).astype(BF), prep[keys, v_lanes]
                        ).astype(BF)

        def feature_block(value, gain_row, target):
            normed, rate = width_norm(value)
            target[at(me, size), :] = (normed * gains[gain_row : gain_row + 1, :]).astype(BF)

        def send_row(buffer):
            return [net.copy(buffer.at[row], buffer.at[row], {"row": peer}) for peer in row_peers]

        top_gathers = []
        top_parts = 4

        def top_start():
            extent = tokens // top_parts
            here = pl.ds(len(top_gathers) * extent, extent)
            top_gathers.append(
                gather_start(
                    lambda at_row, at_col: ref["t0"].at[at_row * cols + at_col, here, :],
                    ("top", len(top_gathers)),
                )
            )

        def top_forward(index):
            for step in range(1, cols):
                gather_step(top_gathers[index], step)

        ref["t0"][me] = og_ref[...].astype(BF)
        top_start()
        top_start()
        row_moves = {}
        last = layers - 1

        def feed_forward(layer, target):
            feat = chip_rows(ref["feat_f"].at[layer], target)
            both = mm(feat, ref["wgu"][layer])
            gate, up = both[:, :ff], both[:, ff:]
            sig = lax.logistic(gate)
            hidden = (gate * sig * up).astype(BF)
            store_rows(ref["hid"].at[layer, row], target, hidden)
            return both, gate, up, sig, hidden

        for layer in range(layers):
            feat_a, feat_f = ref["feat_a"].at[layer], ref["feat_f"].at[layer]
            raw = ref["raw"].at[layer]
            need_weight("wqkv")
            for start in range(0, tokens, 256):
                here = slice(start, start + 256)
                value = mm(feat_a[here, :], ref["wqkv"][layer])
                raw[here, :] = value[:, : head_cols + kv_cols]
                ref["prep"][layer, here, head_cols + kv_cols :] = value[
                    :, head_cols + kv_cols :
                ].astype(BF)
            attend(layer)
            need_weight("wo")

            def compute_o(target, layer=layer):
                return mm(chip_rows(ref["att"].at[layer, row], target), ref["wo"][layer])

            def during_o(layer=layer):
                row_moves["att", layer] = send_row(ref["att"].at[layer])
                if layer == last:
                    top_forward(3)

            total = scatter(compute_o, late, fill_a=during_o)
            if layer == 0:
                for copy in residual_moves:
                    copy.wait()
            ref["res"][2 * layer + 1] = ref["res"][2 * layer] + total
            feature_block(ref["res"][2 * layer + 1], layers + layer, feat_f)
            gathering = gather_start(token_view(feat_f))
            need_weight("wgu")
            need_weight("wd")
            if layer == last:
                break

            def compute_ff(target, layer=layer):
                both, gate, up, sig, hidden = feed_forward(layer, target)
                store_rows(ref["gu"].at[layer], target, both)
                return mm(hidden, ref["wd"][layer])

            def during_ff(layer=layer):
                row_moves["hid", layer] = send_row(ref["hid"].at[layer])

            def idle_ff(layer=layer):
                if layer == 0:
                    top_start()
                    top_forward(0)
                    top_forward(1)

            total = scatter(compute_ff, early, fill_a=during_ff, gather=gathering, idle=idle_ff)
            ref["res"][2 * layer + 2] = ref["res"][2 * layer + 1] + total
            feature_block(ref["res"][2 * layer + 2], layer + 1, ref["feat_a"].at[layer + 1])
            coming = gather_start(token_view(ref["feat_a"].at[layer + 1]))
            for step in range(1, cols):
                gather_step(coming, step)
            if layer == 0:
                top_start()
                top_forward(2)
                grad_moves = to_tokens(og_ref, ref["gtok"])
            for step in range(cols):
                gather_rows(coming, step)
            gather_end(coming)

        window = SUM_WINDOW
        half = dp // 2
        on_left = place < half
        depth = jnp.where(on_left, place, dp - 1 - place)
        inward = jnp.where(on_left, place + 1, place - 1)
        outward = jnp.where(on_left, place - 1, place + 1)
        outward = jnp.clip(outward, 0, dp - 1)
        is_mid = depth == half - 1
        inner = depth > 0

        def views(index):
            name, layer, start, extent = pieces[index]
            rows_at = pl.ds(start, extent)
            return (
                ref["acc_" + name].at[layer, rows_at, :],
                ref["frm_" + name].at[layer, rows_at, :],
                totals[name].at[layer, rows_at, :],
            )

        def hop(source, target, index, kind, peer):
            sems = {
                "up": (up_send, up_recv),
                "across": (up_send, in_recv),
                "back": (in_send, in_recv),
            }[kind]
            return pltpu.make_async_remote_copy(
                src_ref=source,
                dst_ref=target,
                send_sem=sems[0].at[index % window],
                recv_sem=sems[1].at[index],
                device_id={"dp": peer},
                device_id_type=MESH,
            )

        def send_inward(index, condition):
            acc, frm, tot = views(index)

            @pl.when(condition & jnp.logical_not(is_mid))
            def _():
                hop(acc, frm, index, "up", inward).start()

            @pl.when(condition & is_mid)
            def _():
                hop(acc, tot, index, "across", inward).start()

        def add_into(target, one, two):
            extent = one.shape[0]
            chunk = 32

            def body(step, carry):
                here = at(step, chunk)
                target[here, :] = (one[here, :].astype(F32) + two[here, :].astype(F32)).astype(BF)
                return carry

            lax.fori_loop(0, extent // chunk, body, 0)

        def sent_inward(index, condition):
            if index >= 0:
                acc, frm, tot = views(index)

                @pl.when(condition)
                def _():
                    hop(acc, frm, index, "up", inward).wait_send()

        def sent_outward(index, condition):
            if index >= 0:
                tot = views(index)[2]

                @pl.when(condition & inner)
                def _():
                    hop(tot, tot, index, "back", outward).wait_send()

        def up(index):
            sent_inward(index - window, jnp.logical_not(inner))
            send_inward(index, jnp.logical_not(inner))

        def across(index):
            acc, frm, tot = views(index)

            @pl.when(inner)
            def _():
                hop(acc, frm, index, "up", inward).wait_recv()
                add_into(acc, acc, frm)

            sent_inward(index - window, inner)
            send_inward(index, inner)

        def back(index):
            acc, frm, tot = views(index)

            @pl.when(is_mid)
            def _():
                hop(acc, tot, index, "across", inward).wait_recv()
                add_into(tot, acc, tot)

            sent_outward(index - window, is_mid)

            @pl.when(is_mid & inner)
            def _():
                hop(tot, tot, index, "back", outward).start()

        def outer(index):
            acc, frm, tot = views(index)

            @pl.when(jnp.logical_not(is_mid))
            def _():
                hop(tot, tot, index, "back", inward).wait_recv()

            sent_outward(index - window, jnp.logical_not(is_mid))

            @pl.when(jnp.logical_not(is_mid) & inner)
            def _():
                hop(tot, tot, index, "back", outward).start()

        done = {"made": 0, "up": 0, "across": 0, "back": 0}
        ahead_up, ahead_across = 3, 2

        def made(count_new):
            done["made"] += count_new

        def advance(name, action):
            action(done[name])
            done[name] += 1

        def pump(count_steps=1):
            for _ in range(count_steps):
                if done["up"] < done["made"]:
                    advance("up", up)
                    if done["across"] < done["up"] - ahead_up:
                        advance("across", across)
                    if done["back"] < done["across"] - ahead_across:
                        advance("back", back)

        def finish():
            while done["back"] < n_pieces:
                if done["up"] < n_pieces:
                    advance("up", up)
                for _ in range(2):
                    if done["across"] < min(n_pieces, done["up"] - 1 + done["up"] // n_pieces):
                        advance("across", across)
                for _ in range(2):
                    if done["back"] < min(n_pieces, done["across"] - 1 + done["across"] // n_pieces):
                        advance("back", back)
            stores = []
            for index in range(n_pieces):
                outer(index)
                name, layer, start, extent = pieces[index]
                if index + 1 < n_pieces and pieces[index + 1][:2] == (name, layer):
                    continue
                copy = pltpu.make_async_copy(
                    totals[name].at[layer], results[name].at[layer], stored.at[len(stores)]
                )
                copy.start()
                stores.append(copy)
            for copy in stores:
                copy.wait()
            for index in range(n_pieces - window, n_pieces):
                sent_inward(index, depth >= 0)
                sent_outward(index, depth >= 0)

        gb, gb2 = ref["gb"].at[0], ref["gb"].at[1]
        for index in range(top_parts):
            for step in range(cols):
                gather_rows(top_gathers[index], step)
            gather_end(top_gathers[index])
        for slot in range(group):
            gb[:, slot * block : (slot + 1) * block] = ref["t0"][slot]
        gtok, sums = ref["gtok"], ref["sums"]
        for slot in range(group):
            sums[slot] = jnp.zeros((16, HEAD_DIM), F32)

        def slab_of(source):
            return source[:, at(row, slab)]

        quarter = slab // 4

        def slab_part(source, index):
            start = pl.multiple_of(row * slab + index * quarter, quarter)
            return source[:, pl.ds(start, quarter)]

        def norm_back(total, residual, gain_row):
            normed, rate = width_norm(residual)
            scaled = total * gains[gain_row : gain_row + 1, :]
            inner_mean = jnp.mean(scaled * normed, axis=1, keepdims=True)
            gtok[...] = gtok[...] + rate * (scaled - normed * inner_mean)
            line = jnp.sum(total * normed, axis=0, keepdims=True)
            for slot in range(group):
                sums[slot, gain_row : gain_row + 1, :] = line[:, slot * block : (slot + 1) * block]

        def attend_back(layer):
            raw, prep, att = (ref[k].at[layer] for k in ("raw", "prep", "att"))
            inv = ref["inv"]
            gain_q, gain_k = qgain_ref[layer : layer + 1], kgain_ref[layer : layer + 1]
            dqkv, datt = ref["dqkv"], ref["datt"]
            dk, dv, dq = ref["dkv"].at[0], ref["dkv"].at[1], ref["dq"]
            cosine, sine = cos_ref[...], sin_ref[...]
            total_q = jnp.zeros((1, HEAD_DIM), F32)
            total_k = jnp.zeros((1, HEAD_DIM), F32)
            for kv in range(kv_heads):
                k_lanes = slice(head_cols + kv * HEAD_DIM, head_cols + (kv + 1) * HEAD_DIM)
                v_at = head_cols + kv_cols + kv * HEAD_DIM
                v_lanes = slice(v_at, v_at + HEAD_DIM)
                dk[...] = jnp.zeros((tokens, HEAD_DIM), F32)
                dv[...] = jnp.zeros((tokens, HEAD_DIM), F32)
                for member in range(members):
                    head = kv * members + member
                    lanes = slice(head * HEAD_DIM, (head + 1) * HEAD_DIM)
                    lane = layer * q_heads + head
                    for start in range(0, tokens, SEQ_LEN):
                        for begin in range(0, SEQ_LEN, q_block):
                            mine = pl.ds(start + begin, q_block)
                            keys = pl.ds(start, begin + q_block)
                            scores = mm_t(prep[mine, lanes], prep[keys, k_lanes])
                            probs = jnp.exp2(
                                scores * (SCALE * LOG2E)
                                + ref["mask"][mine, 0 : begin + q_block]
                            ) * inv[mine, lane : lane + 1]
                            grad_o = datt[mine, lanes]
                            inner_sum = jnp.sum(
                                grad_o.astype(F32) * att[row, mine, lanes].astype(F32),
                                axis=-1,
                                keepdims=True,
                            )
                            dv[keys, :] += t_mm(probs.astype(BF), grad_o)
                            grad_s = (
                                probs * (mm_t(grad_o, prep[keys, v_lanes]) - inner_sum)
                            ).astype(BF)
                            dq[mine, :] = mm(grad_s, prep[keys, k_lanes]) * SCALE
                            dk[keys, :] += t_mm(grad_s, prep[mine, lanes])
                    back, line = head_back(dq[...], raw[:, lanes], gain_q, cosine, sine)
                    dqkv[row, :, lanes] = back.astype(BF)
                    total_q += line
                back, line = head_back(dk[...] * SCALE, raw[:, k_lanes], gain_k, cosine, sine)
                dqkv[row, :, k_lanes] = back.astype(BF)
                dqkv[row, :, v_lanes] = dv[...].astype(BF)
                total_k += line
            at_row = 8 + 2 * layer
            for slot in range(group):
                sums[slot, at_row : at_row + 1, :] = total_q
                sums[slot, at_row + 1 : at_row + 2, :] = total_k

        for layer in reversed(range(layers)):
            feat_a, feat_f = ref["feat_a"].at[layer], ref["feat_f"].at[layer]
            if layer != last:
                gb[at(me, size), :] = gtok[...].astype(BF)
                gathering = gather_start(token_view(gb))

            def compute_ff_back(target, layer=layer):
                grad = chip_rows(gb, target)
                if layer == last:
                    both, gate, up, sig, hidden = feed_forward(layer, target)
                else:
                    both = chip_rows(ref["gu"].at[layer], target)
                    gate, up = both[:, :ff], both[:, ff:]
                    sig = lax.logistic(gate)
                dhid = mm_t(grad, ref["wd"][layer])
                dgate = (dhid * up * sig * (1.0 + gate * (1.0 - sig))).astype(BF)
                dup = (dhid * gate * sig).astype(BF)
                joined = jnp.concatenate([dgate, dup], axis=1)
                store_rows(ref["dgu"].at[row], target, joined)
                return mm_t(joined, ref["wgu"][layer])

            def down_grads(layer=layer):
                if layer == last:
                    row_moves["hid", layer] = send_row(ref["hid"].at[layer])
                row_moves["dgu"] = send_row(ref["dgu"])
                right = slab_of(gb)
                for step in range(rows):
                    if step == 1:
                        for copy in row_moves.pop(("hid", layer)):
                            copy.wait()
                    there = lax.rem(row + step, rows)
                    ref["acc_down"][layer, at(there, ff), :] = t_mm(
                        ref["hid"][layer, there], right
                    ).astype(BF)
                made(2)
                pump(2)

            def ffn_grads(layer=layer, feat_f=feat_f):
                for copy in row_moves.pop("dgu"):
                    copy.wait()
                for index in range(4):
                    left = slab_part(feat_f, index)
                    here = slice(index * quarter, (index + 1) * quarter)
                    for there in range(rows):
                        value = t_mm(left, ref["dgu"][there]).astype(BF)
                        ref["acc_gu"][layer, here, there * ff : (there + 1) * ff] = value[:, :ff]
                        begin = (rows + there) * ff
                        ref["acc_gu"][layer, here, begin : begin + ff] = value[:, ff:]
                made(4)
                pump()

            total = scatter(
                compute_ff_back, early, fill_a=ffn_grads, gather=gathering, idle=pump,
                between=pump, begin=down_grads,
            )
            if layer == last:
                for copy in grad_moves:
                    copy.wait()
            norm_back(total, ref["res"][2 * layer + 1], layers + layer)
            gb2[at(me, size), :] = gtok[...].astype(BF)
            gathering = gather_start(token_view(gb2))
            pump()
            gather_rest(gathering)
            pump()
            for start in range(0, tokens, 256):
                ref["datt"][start : start + 256, :] = mm_t(
                    gb2[start : start + 256, :], ref["wo"][layer]
                ).astype(BF)
            attend_back(layer)
            pump()
            moves = send_row(ref["dqkv"])

            def compute_qkv_back(target, layer=layer):
                return mm_t(chip_rows(ref["dqkv"].at[row], target), ref["wqkv"][layer])

            def attn_grads(layer=layer, feat_a=feat_a, moves=moves):
                for copy in row_moves.pop(("att", layer)):
                    copy.wait()
                right = slab_of(gb2)
                for there in range(rows):
                    ref["acc_o"][layer, there * head_cols : (there + 1) * head_cols, :] = t_mm(
                        ref["att"][layer, there], right
                    ).astype(BF)
                made(2)
                pump()
                for copy in moves:
                    copy.wait()
                acc = ref["acc_qkv"]
                for index in range(4):
                    left = slab_part(feat_a, index)
                    here = slice(index * quarter, (index + 1) * quarter)
                    for there in range(rows):
                        value = t_mm(left, ref["dqkv"][there]).astype(BF)
                        begin = there * head_cols
                        acc[layer, here, begin : begin + head_cols] = value[:, :head_cols]
                        begin = rows * head_cols + there * kv_cols
                        acc[layer, here, begin : begin + kv_cols] = value[
                            :, head_cols : head_cols + kv_cols
                        ]
                        begin += rows * kv_cols
                        acc[layer, here, begin : begin + kv_cols] = value[:, head_cols + kv_cols :]
                made(4)
                pump()

            total = scatter(compute_qkv_back, late, fill_a=attn_grads, between=pump)
            norm_back(total, ref["res"][2 * layer], layer)
            pump()

        sums_in, dsum = ref["sums_in"], ref["dsum"]
        sum_moves = []
        for there in others:
            index = there[0] * cols + there[1]
            sum_moves.append(
                net.copy(sums.at[index], sums_in.at[me], {"row": there[0], "col": there[1]})
            )
        sums_in[me] = sums[me]
        din_moves = to_features(gtok, din_ref)

        def compute_down(target):
            return mm(chip_rows(ref["hid"].at[last, row], target), ref["wd"][last])

        pump()
        result = scatter(compute_down, late, slots=1)
        ref["fin"][...] = ref["res"][2 * last + 1] + result
        out_moves = to_features(ref["fin"], out_ref)
        for copy in sum_moves:
            copy.wait()
        total = sums_in[0]
        for slot in range(1, group):
            total += sums_in[slot]
        dsum[place] = total
        sum_moves = [
            net.copy(dsum.at[place], dsum.at[place], {"dp": lax.rem(place + step, dp)})
            for step in range(1, dp)
        ]
        for copy in din_moves + out_moves:
            copy.wait()
        for copy in sum_moves:
            copy.wait()
        total = dsum[0]
        for slot in range(1, dp):
            total += dsum[slot]
        small_ref[...] = total
        finish()

    def call(*operands):
        shapes_out = [
            jax.ShapeDtypeStruct((tokens, block), F32),
            jax.ShapeDtypeStruct((tokens, block), F32),
            jax.ShapeDtypeStruct((16, HEAD_DIM), F32),
        ] + [jax.ShapeDtypeStruct(grad_shapes[name], BF) for name in grad_names]
        return pl.pallas_call(
            kernel,
            name="layers",
            out_shape=shapes_out,
            in_specs=[VM] * 7 + [ANY] * 7,
            out_specs=[VM] * 3 + [ANY] * len(grad_names),
            scratch_shapes=[pltpu.VMEM(*scratch[name]) for name in names]
            + [
                pltpu.SemaphoreType.DMA((limit,)),
                pltpu.SemaphoreType.DMA((limit,)),
                pltpu.SemaphoreType.DMA((7,)),
            ]
            + [
                pltpu.SemaphoreType.DMA((extent,))
                for extent in (
                    SUM_WINDOW, n_pieces, SUM_WINDOW, n_pieces, len(grad_names) * layers,
                )
            ],
            compiler_params=pltpu.CompilerParams(
                collective_id=1, has_side_effects=True, vmem_limit_bytes=60 << 20
            ),
        )(*operands)

    return call


def per_device(
    sizes,
    residual_in,
    positions,
    attn_gain,
    query_weight,
    key_weight,
    value_weight,
    query_gain,
    key_gain,
    output_weight,
    ffn_gain,
    gate_weight,
    up_weight,
    down_weight,
    output_grad,
):
    dp, rows, cols = sizes
    layers = query_weight.shape[0]
    tokens, block = residual_in.shape
    shapes = (
        layers, tokens, block, query_weight.shape[2] // rows, key_weight.shape[2] // rows,
        gate_weight.shape[2] // rows,
    )
    outputs, input_grad, small, down, gu, out_w, qkv = layers_kernel(sizes, shapes)(
        residual_in, output_grad, attn_gain, ffn_gain, query_gain, key_gain,
        positions.reshape(tokens // 128, 128),
        query_weight, key_weight, value_weight, output_weight, gate_weight, up_weight, down_weight,
    )
    return widen(
        outputs, input_grad, small, down, gu, out_w, qkv,
        (query_weight.shape[2], key_weight.shape[2], gate_weight.shape[2]),
    )


def widen(outputs, input_grad, small, down, gu, out_w, qkv, columns):
    wide_q, wide_k, wide_f = columns
    layers, parts = down.shape[0], 2
    tokens, block = outputs.shape

    def kernel(
        out_in, din_in, small_in, down_in, gu_in, o_in, qkv_in,
        out_ref, din_ref, again_ref, q_ref, k_ref, v_ref, qgain_ref, kgain_ref, o_ref, fgain_ref,
        gate_ref, up_ref, down_ref,
    ):
        out_ref[...] = out_in[...]
        din_ref[...] = din_in[...]
        again_ref[...] = small_in[0:layers, :]
        fgain_ref[...] = small_in[layers : 2 * layers, :]
        for layer in range(layers):
            start = 8 + 2 * layer
            qgain_ref[layer : layer + 1, :] = small_in[start : start + 1, :]
            kgain_ref[layer : layer + 1, :] = small_in[start + 1 : start + 2, :]
        q_ref[...] = qkv_in[:, :, :wide_q].astype(F32)
        k_ref[...] = qkv_in[:, :, wide_q : wide_q + wide_k].astype(F32)
        v_ref[...] = qkv_in[:, :, wide_q + wide_k :].astype(F32)
        o_ref[...] = o_in[...].astype(F32)
        gate_ref[...] = gu_in[:, :, :wide_f].astype(F32)
        up_ref[...] = gu_in[:, :, wide_f:].astype(F32)
        down_ref[...] = down_in[...].astype(F32)

    flat = pl.BlockSpec((tokens // (layers * parts), block), lambda i, j: (i * parts + j, 0))

    def whole(shape):
        return pl.BlockSpec(shape, lambda i, j: (0,) * len(shape))

    def cut(height, width):
        return pl.BlockSpec((1, height // parts, width), lambda i, j: (i, j, 0))

    def shape_of(*extent):
        return jax.ShapeDtypeStruct(extent, F32)

    slab, wide_d = qkv.shape[1], down.shape[1]
    wide_o, out_cols = out_w.shape[1:]
    gain = (layers, block)
    head_gain = (layers, HEAD_DIM)
    return pl.pallas_call(
        kernel,
        name="widen",
        grid=(layers, parts),
        in_specs=[
            flat, flat, whole(small.shape), cut(wide_d, out_cols), cut(slab, gu.shape[2]),
            cut(wide_o, out_cols), cut(slab, qkv.shape[2]),
        ],
        out_specs=[
            flat, flat, whole(gain), cut(slab, wide_q), cut(slab, wide_k), cut(slab, wide_k),
            whole(head_gain), whole(head_gain), cut(wide_o, out_cols), whole(gain),
            cut(slab, wide_f), cut(slab, wide_f), cut(wide_d, out_cols),
        ],
        out_shape=[
            shape_of(tokens, block), shape_of(tokens, block), shape_of(*gain),
            shape_of(layers, slab, wide_q), shape_of(layers, slab, wide_k),
            shape_of(layers, slab, wide_k), shape_of(*head_gain), shape_of(*head_gain),
            shape_of(layers, wide_o, out_cols), shape_of(*gain),
            shape_of(layers, slab, wide_f), shape_of(layers, slab, wide_f),
            shape_of(layers, wide_d, out_cols),
        ],
        compiler_params=pltpu.CompilerParams(vmem_limit_bytes=60 << 20),
    )(outputs, input_grad, small, down, gu, out_w, qkv)


def solution(mesh):
    wide = P("dp", ("row", "col"))
    gain = P(None, ("row", "col"))
    into, out_of = P(None, "row", "col"), P(None, "col", "row")
    in_specs = (
        wide, P("dp"), gain, into, into, into, P(), P(), out_of, gain, into, into, out_of, wide,
    )
    out_specs = (wide, wide, gain, into, into, into, P(), P(), out_of, gain, into, into, out_of)
    return jax.shard_map(
        functools.partial(per_device, (mesh.shape["dp"], mesh.shape["row"], mesh.shape["col"])),
        mesh=mesh,
        in_specs=in_specs,
        out_specs=out_specs,
        check_vma=False,
    )
```
